512 devices in a mesh: sec: 128 (over z, y, x_hi), col: 4 (over x_lo, core).
Axes of the slice: x: 4 (x_hi: 2, x_lo: 2; x = x_hi * 2 + x_lo), y: 8, z: 8, core: 2. Of those that a mesh axis runs over, the one named last changes fastest.
Arguments:
- positions: float32 [2, 128, 512, 512], P(None, 'sec', None, 'col'), may hold values from -18 to 18
- initial_velocity: float32 [2, 128, 512, 512], P(None, 'sec', None, 'col'), may hold values from -6 to 6
- flow: float32 [2, 128, 512, 512], P(None, 'sec', None, 'col'), may hold values from -3 to 3
- valid: int32 [128, 512, 512], P('sec', None, 'col'), may hold values 0 or 1
- step_sizes: float32 [4], replicated, may hold values from 0.05 to 0.15
- mixing: float32 [4], replicated, may hold values from 0.1 to 0.4
- resets: int32 [4], replicated, may hold values from 0 to 1
Outputs:
- final_positions: float32 [2, 128, 512, 512], P(None, 'sec', None, 'col')
- final_velocity: float32 [2, 128, 512, 512], P(None, 'sec', None, 'col')
- power: float32 [4], replicated
The draws below stay inside these ranges and needn't reach their ends.
All inputs are finite; a program needn't handle non-finite values. No bound on the sum of `valid` on one device may be relied on, other than what follows from the above.
Results may differ from the reference program's by a relative error of at most 0.0001.
Values sent between devices are 32-bit elements; how exact they have to be, the bound alone decides.
No kernel may reach another device: no remote copies, remote signals or barrier semaphores. Data moves between devices by JAX's collectives and lax.ppermute only.
A program may use at most 64 MiB of HBM per device.

```python
import jax
import jax.numpy as jnp

SEC_DEV = 1
ROWS = 512
COLS = 512
STEPS = 4
SECTIONS = 128


def draw_positions(key, part):
    sec_index = jnp.arange(SECTIONS).astype(jnp.float32)
    ratio = (sec_index / max(SECTIONS - 1, 1)).reshape(1, -1, 1, 1)
    shape = (2, SECTIONS, ROWS, COLS)
    base = jnp.clip(jax.random.normal(key, shape, jnp.float32), -6.0, 6.0)
    return base * (1.0 + 2.0 * ratio)


def draw_resets(key, part):
    code_key = jax.random.fold_in(key, 23)
    first_bit = jnp.zeros((1,), jnp.int32)
    code = jax.random.randint(code_key, (), 1, 2 ** (STEPS - 1) - 1).astype(jnp.int32)
    shifts = jnp.arange(STEPS - 1).astype(jnp.int32)
    later = jnp.right_shift(code, shifts) % 2
    return jnp.concatenate([first_bit, later.astype(jnp.int32)], axis=0)


def place_ends(values, own_key, least, high):
    spot = [jax.random.randint(jax.random.fold_in(own_key, axis), (), 0, length) for axis, length in enumerate(values.shape)]
    main_axis = values.shape.index(max(values.shape))
    neighbour = spot[:main_axis] + [(spot[main_axis] + 1) % values.shape[main_axis]] + spot[main_axis + 1:]
    return values.at[tuple(spot)].set(least).at[tuple(neighbour)].set(high)


def block_scale(rng, extent, split, least, largest):
    def one(dim, blocks):
        heights = jax.random.uniform(jax.random.fold_in(jax.random.fold_in(rng, 6), dim), (blocks,), jnp.float32, least / len(split), largest / len(split))
        return jnp.repeat(jnp.exp(heights), extent[dim] // blocks).reshape((-1,) + (1,) * (len(extent) - dim - 1))

    level = one(*split[0])
    for cut in split[1:]:
        level = level * one(*cut)
    return level


def noise(rng, dims, width, most, cuts=(), dtype=jnp.bfloat16):
    drawn = width * jax.random.normal(rng, dims, jnp.float32)
    if cuts:
        drawn = drawn * block_scale(rng, dims, cuts, -0.22, 0.18)
    return jnp.clip(drawn, -most, most).astype(dtype)


def setup_inputs(seed: int = 0) -> dict:
    keys = jax.random.split(jax.random.key(seed), 8)
    positions = draw_positions(jax.random.fold_in(keys[7], 71), 0)
    initial_velocity = noise(keys[1], (2, SECTIONS, ROWS, COLS), 1.0, 6.0, ((1, 128), (3, 4)), jnp.float32)
    flow = noise(keys[2], (2, SECTIONS, ROWS, COLS), 0.5, 3.0, ((1, 128), (3, 4)), jnp.float32)
    valid = place_ends((jax.random.randint(keys[3], (SECTIONS, ROWS, COLS), 0, 4) < 3).astype(jnp.int32), jax.random.fold_in(keys[3], 1), 0, 1)
    step_sizes = jnp.clip(jax.random.uniform(keys[4], (STEPS,), jnp.float32, 0.05, 0.15), 0.05, 0.15)
    mixing = jnp.clip(jax.random.uniform(keys[5], (STEPS,), jnp.float32, 0.1, 0.4), 0.1, 0.4)
    resets = draw_resets(jax.random.fold_in(keys[7], 71), 0)
    return dict(positions=positions, initial_velocity=initial_velocity, flow=flow, valid=valid, step_sizes=step_sizes, mixing=mixing, resets=resets)


K_INNER = 1.0
K_CROSS = 0.5
EPS = 1e-06

def inner_force(field):
    row_diff = field[:, :, 1:, :] - field[:, :, :-1, :]
    col_diff = field[:, :, :, 1:] - field[:, :, :, :-1]
    zero_row = ((0, 0), (0, 0), (0, 1), (0, 0))
    one_row = ((0, 0), (0, 0), (1, 0), (0, 0))
    zero_col = ((0, 0), (0, 0), (0, 0), (0, 1))
    one_col = ((0, 0), (0, 0), (0, 0), (1, 0))
    total = jnp.pad(row_diff, zero_row) - jnp.pad(row_diff, one_row)
    total = total + jnp.pad(col_diff, zero_col) - jnp.pad(col_diff, one_col)
    return K_INNER * total

def reference(positions, initial_velocity, flow, valid, step_sizes, mixing, resets):
    count = positions.shape[1]
    sec_index = jnp.arange(count)
    first_block = (sec_index % SEC_DEV == 0)[None, :, None, None]
    last_block = ((sec_index + 1) % SEC_DEV == 0)[None, :, None, None]
    valid_float = valid.astype(jnp.float32)
    low_mask = (valid_float * (sec_index > 0).astype(jnp.float32)[:, None, None])[None]
    empty_one = jnp.zeros_like(valid_float[:1])
    up_mask = jnp.concatenate([valid_float[1:], empty_one], axis=0)[None]
    empty_two = jnp.zeros_like(flow[:, :1])
    up_flow = jnp.concatenate([flow[:, 1:], empty_two], axis=1)

    def shift_down(field):
        return jnp.concatenate([jnp.zeros_like(field[:, :1]), field[:, :-1]], axis=1)

    def shift_up(field):
        return jnp.concatenate([field[:, 1:], jnp.zeros_like(field[:, :1])], axis=1)
    current = positions
    lagged = positions
    velocity = initial_velocity
    powers = []
    for iteration in range(STEPS):
        below = jnp.where(first_block, shift_down(lagged), shift_down(current))
        above = jnp.where(last_block, shift_up(lagged), shift_up(current))
        forces = inner_force(current) + K_CROSS * (low_mask * (below + flow - current) + up_mask * (above - up_flow - current))
        power_now = jnp.sum(forces * velocity)
        force_sq = jnp.sum(forces * forces)
        speed_sq = jnp.sum(velocity * velocity)
        powers.append(power_now)
        scale = mixing[iteration] * jnp.sqrt(speed_sq / (force_sq + EPS))
        keep_rate = 1.0 - resets[iteration].astype(jnp.float32)
        velocity = keep_rate * ((1.0 - mixing[iteration]) * velocity + scale * forces) + step_sizes[iteration] * forces
        lagged = current
        current = current + step_sizes[iteration] * velocity
    return (current, velocity, jnp.stack(powers))
```

```python
import jax
import jax.numpy as jnp
from jax import lax
from jax.sharding import Mesh, PartitionSpec as P

STEPS = 4

K_INNER = 1.0
K_CROSS = 0.5
EPS = 1e-06

SEC = ("z", "y", "xh")
COL = ("xl", "core")


def from_behind(block, distance):
    count = lax.axis_size(SEC)
    route = [(i - distance, i) for i in range(count) if 0 <= i - distance < count]
    return lax.ppermute(block, SEC, route)


def total_over(rows, axes):
    count = lax.axis_size(axes)
    sent = lax.optimization_barrier(jnp.broadcast_to(rows, (count, rows.shape[-1])))
    got = lax.all_to_all(sent, axes, 0, 0, tiled=True)
    return jnp.sum(got, axis=0, keepdims=True)


def all_sums(*terms):
    row = jnp.zeros((1, 128), jnp.float32)
    for place, term in enumerate(terms):
        row = row.at[0, place].set(term)
    row = total_over(row, ("z", "xh", "xl"))
    row = total_over(row, ("y", "core"))
    return [row[0, place] for place in range(len(terms))]


def edge_column(column, forward):
    count = lax.axis_size(COL)
    pairs = [(i, i + 1) for i in range(count - 1)]
    if not forward:
        pairs = [(b, a) for a, b in pairs]
    packed = column.reshape(8, 128)
    return lax.ppermute(packed, COL, pairs).reshape(column.shape)


def inner_force(field):
    row_diff = field[:, :, 1:, :] - field[:, :, :-1, :]
    zero_row = ((0, 0), (0, 0), (0, 1), (0, 0))
    one_row = ((0, 0), (0, 0), (1, 0), (0, 0))
    total = jnp.pad(row_diff, zero_row) - jnp.pad(row_diff, one_row)
    low = edge_column(field[..., -1:], True)
    high = edge_column(field[..., :1], False)
    padded = jnp.concatenate([low, field, high], axis=3)
    width = field.shape[3]
    col_index = jnp.arange(width)
    col_pos = lax.axis_index(COL)
    left_keep = ((col_index > 0) | (col_pos > 0)).astype(jnp.float32)
    right_keep = ((col_index < width - 1) | (col_pos < lax.axis_size(COL) - 1)).astype(
        jnp.float32
    )
    total = total + left_keep * (padded[..., :-2] - field) + right_keep * (padded[..., 2:] - field)
    return K_INNER * total


def per_device(positions, initial_velocity, flow, valid, step_sizes, mixing, resets):
    valid_float = valid.astype(jnp.float32)[None]
    bottom_keep = jnp.where(lax.axis_index(SEC) == 0, 0.0, 1.0).astype(jnp.float32)
    low_mask = valid_float * bottom_keep
    up_mask = from_behind(valid_float, -1)
    current = positions
    lagged = positions
    velocity = initial_velocity
    powers = []
    for iteration in range(STEPS):
        below = from_behind(lagged, 1)
        above = from_behind(valid_float * (lagged - flow), -1)
        forces = inner_force(current) + K_CROSS * (
            low_mask * (below + flow - current) + (above - up_mask * current)
        )
        power_now, force_sq, speed_sq = all_sums(
            jnp.sum(forces * velocity), jnp.sum(forces * forces), jnp.sum(velocity * velocity)
        )
        powers.append(power_now)
        scale = mixing[iteration] * jnp.sqrt(speed_sq / (force_sq + EPS))
        keep_rate = 1.0 - resets[iteration].astype(jnp.float32)
        velocity = (
            keep_rate * ((1.0 - mixing[iteration]) * velocity + scale * forces)
            + step_sizes[iteration] * forces
        )
        lagged = current
        current = current + step_sizes[iteration] * velocity
    return (current, velocity, jnp.stack(powers))


def solution(mesh):
    fine = Mesh(mesh.devices.reshape(8, 8, 2, 2, 2), SEC + COL)
    field = P(None, SEC, None, COL)
    return jax.shard_map(
        per_device,
        mesh=fine,
        in_specs=(field, field, field, P(SEC, None, COL), P(), P(), P()),
        out_specs=(field, field, P()),
        check_vma=False,
    )
```

```python
import functools

import jax
import jax.numpy as jnp
from jax import lax
from jax.experimental import pallas as pl
from jax.experimental.pallas import tpu as pltpu
from jax.sharding import Mesh, PartitionSpec as P


K_INNER = 1.0
K_CROSS = 0.5
EPS = 1e-06

SEC = ("z", "y", "xh")
COL = ("xl", "core")
PAIR = ("z", "y")
TEAM = ("xh", "xl", "core")
FIRST = ("z", "xh", "xl")
SECOND = ("y", "core")

OWN = 64
ROWS = 72
LANES = 128
TEAMS = 8
BLOCKS = 4


def roll(x, shift, axis):
    return pltpu.roll(x, shift % x.shape[axis], axis)


def lane_of(x):
    return lax.broadcasted_iota(jnp.int32, x.shape, len(x.shape) - 1)


def laplacian(tiles, j):
    x = tiles[j]
    lane = lane_of(x)
    before = roll(x, 1, 0)
    after = roll(x, -1, 0)
    if j == 0:
        left = jnp.where(lane == 0, x, roll(x, 1, 1))
    else:
        left = roll(jnp.where(lane == LANES - 1, tiles[j - 1], x), 1, 1)
    if j == BLOCKS - 1:
        right = jnp.where(lane == LANES - 1, x, roll(x, -1, 1))
    else:
        right = roll(jnp.where(lane == 0, tiles[j + 1], x), -1, 1)
    return K_INNER * (((before - x) + (after - x)) + ((left - x) + (right - x)))


def mirror(tile):
    row = lax.broadcasted_iota(jnp.int32, tile.shape, 0)
    tile = roll(tile, 4, 0)
    tile = jnp.where(row % 4 < 2, roll(tile, -2, 0), roll(tile, 2, 0))
    return jnp.where(row % 2 < 1, roll(tile, -1, 0), roll(tile, 1, 0))


def pack_kernel(u_ref, v_ref, flow_ref, valid_ref, first_ref, second_ref):
    lowest = (
        lax.axis_index("z") + lax.axis_index("y") + lax.axis_index("xh") == 0
    )
    strength = jnp.where(lowest, 0.0, K_CROSS).astype(jnp.float32)

    def planes(rows):
        u = [u_ref[comp, 0, rows] for comp in range(2)]
        c = valid_ref[0, rows].astype(jnp.float32) * strength
        w = [c * (u[comp] - flow_ref[comp, 0, rows]) for comp in range(2)]
        v = [v_ref[comp, 0, rows] for comp in range(2)]
        return u + w + [c] + v

    def put(q, rows, values):
        for place, value in enumerate(values):
            if place < 5:
                first_ref[q, place, rows] = value
            else:
                second_ref[q, place - 5, rows] = value

    for q in range(TEAMS):
        put(q, pl.ds(0, OWN), planes(pl.ds(q * OWN, OWN)))
        if q == TEAMS - 1:
            after = [mirror(x) for x in planes(pl.ds(TEAMS * OWN - 8, 8))]
        else:
            after = planes(pl.ds(q * OWN + OWN, 8))
        if q == 0:
            before = [mirror(x) for x in planes(pl.ds(0, 8))]
        else:
            before = planes(pl.ds(q * OWN - 8, 8))
        row = lax.broadcasted_iota(jnp.int32, (8, LANES), 0)
        halo = [jnp.where(row < 4, x, y) for x, y in zip(after, before)]
        put(q, pl.ds(OWN, 8), halo)


def rates(par, t):
    dt_ref, mix_ref, reset_ref = par
    keep = 1.0 - reset_ref[t].astype(jnp.float32)
    return dt_ref[t], keep * (1.0 - mix_ref[t]), keep * mix_ref[t]


def fold(x, y):
    return jnp.sum((x[:OWN] * y[:OWN]).reshape(OWN // 8, 8, LANES), axis=0)


def pairs_of(v, f, g, h):
    return [(f, v), (f, f), (v, v), (g, v), (g, f), (h, v), (h, f), (g, g), (g, h), (h, h)]


def put_sums(sums, out_ref):
    lane = lax.broadcasted_iota(jnp.int32, (8, LANES), 1)
    row = jnp.zeros((8, LANES), jnp.float32)
    for place, part in enumerate(sums):
        row = jnp.where(lane == place, jnp.sum(part, axis=(0, 1), keepdims=True), row)
    count = min(out_ref.shape[0], 8)
    for start in range(0, out_ref.shape[0], count):
        out_ref[pl.ds(start, count)] = row[:count]


def two_steps(total_ref, par, t):
    total = jnp.sum(total_ref[...], axis=0, keepdims=True)
    fv, ff, vv, gv, gf, hv, hf, gg, gh, hh = [total[:, i : i + 1] for i in range(10)]
    dt, a, m = rates(par, t)
    b = m * jnp.sqrt(vv / (ff + EPS)) + dt
    dt_next, a_next, m_next = rates(par, t + 1)
    power_next = a * gv + b * gf + b * (a * hv + b * hf)
    ff_next = jnp.maximum(gg + b * (2.0 * gh + b * hh), 0.0)
    vv_next = jnp.maximum(a * a * vv + b * (2.0 * a * fv + b * ff), 0.0)
    b_next = m_next * jnp.sqrt(vv_next / (ff_next + EPS)) + dt_next
    return (dt, a, b), (dt_next, a_next, b_next), (fv, power_next)


def start_kernel(dt_ref, mix_ref, reset_ref, r1, r2, up, dn, fa, fb, sums_ref):
    par = (dt_ref, mix_ref, reset_ref)
    fields = (fa, fb)
    dt, a, _ = rates(par, 0)

    def cross(s, j):
        return dn[j, 2] if s == 2 else r1[4 * s + j, 4]

    def weighted(s, comp, j):
        return dn[j, comp] if s == 2 else r1[4 * s + j, 2 + comp]

    for comp in range(2):
        for s in range(2):
            u = [r1[4 * s + j, comp] for j in range(BLOCKS)]
            for j in range(BLOCKS):
                below = up[j, comp] if s == 0 else r1[j, comp]
                fields[s][1, comp, j] = (
                    laplacian(u, j)
                    + (cross(s, j) * below - weighted(s, comp, j))
                    + (weighted(s + 1, comp, j) - cross(s + 1, j) * u[j])
                )
    sums = [jnp.zeros((8, LANES), jnp.float32)] * 10
    for comp in range(2):
        for s in range(2):
            v = [r2[4 * s + j, comp] for j in range(BLOCKS)]
            f = [fields[s][1, comp, j] for j in range(BLOCKS)]
            for j in range(BLOCKS):
                diag = cross(s, j) + cross(s + 1, j)
                g = f[j] + (dt * a) * (laplacian(v, j) - diag * v[j])
                h = dt * (laplacian(f, j) - diag * f[j])
                fields[s][0, comp, j] = v[j]
                fields[s][2, comp, j] = g
                fields[s][3, comp, j] = h
                sums = [t + fold(x, y) for t, (x, y) in zip(sums, pairs_of(v[j], f[j], g, h))]
    put_sums(sums, sums_ref)


def middle_kernel(
    dt_ref, mix_ref, reset_ref, total_ref, r1, dn, fa, fb, na, nb, out_ref, sums_ref, power_ref, v1s, v2s, f2s
):
    par = (dt_ref, mix_ref, reset_ref)
    (dt0, a0, b0), (dt1, a1, b1), powers = two_steps(total_ref, par, 0)
    dt2, a2, _ = rates(par, 2)
    lane = lax.broadcasted_iota(jnp.int32, (8, LANES), 1)
    power_ref[...] = jnp.where(lane == 0, powers[0], powers[1])

    def cross(s, j):
        return dn[j, 2] if s == 2 else r1[4 * s + j, 4]

    sums = [jnp.zeros((8, LANES), jnp.float32)] * 10
    for comp in range(2):
        for place, field in enumerate((nb, fa, fb, na)):
            for j in range(BLOCKS):
                v1 = a0 * field[0, comp, j] + b0 * field[1, comp, j]
                f1 = field[2, comp, j] + b0 * field[3, comp, j]
                v1s[place, j] = v1
                v2s[place, j] = a1 * v1 + b1 * f1
                if place in (1, 2):
                    f2s[place - 1, j] = f1
        for s in range(2):
            v = [v2s[s + 1, j] for j in range(BLOCKS)]
            for j in range(BLOCKS):
                low, high = cross(s, j), cross(s + 1, j)
                own = laplacian(v, j) - (low + high) * v[j]
                f2 = (f2s[s, j] + dt1 * own) + dt0 * (low * v1s[s, j] + high * v1s[s + 2, j])
                g = (f2 + (dt2 * a2) * own) + dt1 * (low * v2s[s, j] + high * v2s[s + 2, j])
                f2s[s, j] = f2
                out_ref[2, s, comp, j] = g[:OWN]
            f = [f2s[s, j] for j in range(BLOCKS)]
            for j in range(BLOCKS):
                diag = cross(s, j) + cross(s + 1, j)
                h = dt2 * (laplacian(f, j) - diag * f[j])
                v2 = v2s[s + 1, j]
                out_ref[0, s, comp, j] = v2[:OWN]
                out_ref[1, s, comp, j] = f[j][:OWN]
                out_ref[3, s, comp, j] = h[:OWN]
                out_ref[4, s, comp, j] = (
                    r1[4 * s + j, comp] + dt0 * v1s[s + 1, j] + dt1 * v2
                )[:OWN]
                g = out_ref[2, s, comp, j]
                sums = [t + fold(x, y) for t, (x, y) in zip(sums, pairs_of(v2, f[j], g, h))]
    put_sums(sums, sums_ref)


def end_kernel(dt_ref, mix_ref, reset_ref, total_ref, power_ref, in_ref, out_ref, all_power_ref):
    par = (dt_ref, mix_ref, reset_ref)
    (dt2, a2, b2), (dt3, a3, b3), powers = two_steps(total_ref, par, 2)
    for place, power in enumerate((power_ref[0:1, 0:1], power_ref[0:1, 1:2]) + powers):
        all_power_ref[place] = power[0, 0]
    for s in range(2):
        for comp in range(2):
            for j in range(BLOCKS):
                v2, f2, g, h, u2 = [in_ref[i, s, comp, j] for i in range(5)]
                v3 = a2 * v2 + b2 * f2
                v4 = a3 * v3 + b3 * (g + b2 * h)
                out_ref[4 * s + j, comp] = (u2 + dt2 * v3) + dt3 * v4
                out_ref[4 * s + j, 2 + comp] = v4


def unpack_kernel(in_ref, u_ref, v_ref):
    for q in range(TEAMS):
        for comp in range(2):
            u_ref[comp, 0, pl.ds(q * OWN, OWN)] = in_ref[q, comp]
            v_ref[comp, 0, pl.ds(q * OWN, OWN)] = in_ref[q, 2 + comp]


def call(kernel, outs, *args, scalars=0, scratch=(), scalar_outs=()):
    smem = pl.BlockSpec(memory_space=pltpu.SMEM)
    vmem = pl.BlockSpec(memory_space=pltpu.VMEM)
    moved = sum(x.size for x in args) * 4 + sum(functools.reduce(lambda p, n: p * n, o, 1) for o in outs) * 4
    return pl.pallas_call(
        kernel,
        out_shape=[jax.ShapeDtypeStruct(o, jnp.float32) for o in outs],
        in_specs=[smem] * scalars + [vmem] * (len(args) - scalars),
        out_specs=[smem if i in scalar_outs else vmem for i in range(len(outs))],
        scratch_shapes=[pltpu.VMEM(s, jnp.float32) for s in scratch],
        cost_estimate=pl.CostEstimate(flops=moved * 8, bytes_accessed=moved, transcendentals=0),
        compiler_params=pltpu.CompilerParams(vmem_limit_bytes=40 * 1024 * 1024),
    )(*args)


def exchange(x, axes):
    return lax.all_to_all(x, axes, 0, 0, tiled=True)


def upward(x):
    count = lax.axis_size(PAIR)
    return lax.ppermute(x, PAIR, [(i, i + 1) for i in range(count - 1)])


def downward(x):
    count = lax.axis_size(PAIR)
    return lax.ppermute(x, PAIR, [(i + 1, i) for i in range(count - 1)])


def all_sums(rows):
    got = exchange(rows, FIRST)
    count = lax.axis_size(SECOND)
    row = jnp.sum(got, axis=0, keepdims=True)
    return exchange(lax.optimization_barrier(jnp.broadcast_to(row, (count, LANES))), SECOND)


def per_device(positions, initial_velocity, flow, valid, step_sizes, mixing, resets):
    par = (step_sizes, mixing, resets)
    peers = lax.axis_size(FIRST)
    first, second = call(
        pack_kernel,
        [(TEAMS, 5, ROWS, LANES), (TEAMS, 2, ROWS, LANES)],
        positions,
        initial_velocity,
        flow,
        valid,
    )
    r1 = exchange(first, TEAM)
    up = upward(r1[4:, :2])
    dn = downward(r1[:4, 2:])
    r2 = exchange(second, TEAM)
    field = (4, 2, BLOCKS, ROWS, LANES)
    fa, fb, sums = call(start_kernel, [field, field, (peers, LANES)], *par, r1, r2, up, dn, scalars=3)
    nb = upward(fb)
    na = downward(fa)
    total = all_sums(sums)
    state, sums, powers = call(
        middle_kernel,
        [(5, 2, 2, BLOCKS, OWN, LANES), (peers, LANES), (8, LANES)],
        *par,
        total,
        r1,
        dn,
        fa,
        fb,
        na,
        nb,
        scalars=3,
        scratch=[(4, BLOCKS, ROWS, LANES), (4, BLOCKS, ROWS, LANES), (2, BLOCKS, ROWS, LANES)],
    )
    total = all_sums(sums)
    packed, power = call(
        end_kernel,
        [(TEAMS, 4, OWN, LANES), (4,)],
        *par,
        total,
        powers,
        state,
        scalars=3,
        scalar_outs=(1,),
    )
    back = exchange(packed, TEAM)
    shape = positions.shape
    final_positions, final_velocity = call(unpack_kernel, [shape, shape], back)
    return final_positions, final_velocity, power


def on_mesh(fine):
    field = P(None, SEC, None, COL)
    return jax.shard_map(
        per_device,
        mesh=fine,
        in_specs=(field, field, field, P(SEC, None, COL), P(), P(), P()),
        out_specs=(field, field, P()),
        check_vma=False,
    )


def solution(mesh):
    return on_mesh(Mesh(mesh.devices.reshape(8, 8, 2, 2, 2), SEC + COL))
```

```python
import functools

import jax
import jax.numpy as jnp
from jax import lax
from jax.experimental import pallas as pl
from jax.experimental.pallas import tpu as pltpu
from jax.sharding import Mesh, PartitionSpec as P


K_INNER = 1.0
K_CROSS = 0.5
EPS = 1e-06

SEC = ("z", "y", "xh")
COL = ("xl", "core")
PAIR = ("z", "y")
TEAM = ("xh", "xl", "core")
FIRST = ("z", "xh", "xl")
SECOND = ("y", "core")

OWN = 64
ROWS = 72
LANES = 128
TEAMS = 8
BLOCKS = 4


def roll(x, shift, axis):
    return pltpu.roll(x, shift % x.shape[axis], axis)


def lane_of(x):
    return lax.broadcasted_iota(jnp.int32, x.shape, len(x.shape) - 1)


def laplacian(tiles, j):
    x = tiles[j]
    lane = lane_of(x)
    before = roll(x, 1, 0)
    after = roll(x, -1, 0)
    if j == 0:
        left = jnp.where(lane == 0, x, roll(x, 1, 1))
    else:
        left = roll(jnp.where(lane == LANES - 1, tiles[j - 1], x), 1, 1)
    if j == BLOCKS - 1:
        right = jnp.where(lane == LANES - 1, x, roll(x, -1, 1))
    else:
        right = roll(jnp.where(lane == 0, tiles[j + 1], x), -1, 1)
    return K_INNER * (((before - x) + (after - x)) + ((left - x) + (right - x)))


def mirror(tile):
    row = lax.broadcasted_iota(jnp.int32, tile.shape, 0)
    tile = roll(tile, 4, 0)
    tile = jnp.where(row % 4 < 2, roll(tile, -2, 0), roll(tile, 2, 0))
    return jnp.where(row % 2 < 1, roll(tile, -1, 0), roll(tile, 1, 0))


def pack_kernel(u_ref, v_ref, flow_ref, valid_ref, first_ref, second_ref):
    lowest = (
        lax.axis_index("z") + lax.axis_index("y") + lax.axis_index("xh") == 0
    )
    strength = jnp.where(lowest, 0.0, K_CROSS).astype(jnp.float32)

    def planes(rows):
        u = [u_ref[comp, 0, rows] for comp in range(2)]
        c = valid_ref[0, rows].astype(jnp.float32) * strength
        w = [c * (u[comp] - flow_ref[comp, 0, rows]) for comp in range(2)]
        v = [v_ref[comp, 0, rows] for comp in range(2)]
        return u + w + [c] + v

    def put(q, rows, values):
        for place, value in enumerate(values):
            if place < 5:
                first_ref[q, place, rows] = value
            else:
                second_ref[q, place - 5, rows] = value

    for q in range(TEAMS):
        put(q, pl.ds(0, OWN), planes(pl.ds(q * OWN, OWN)))
        if q == TEAMS - 1:
            after = [mirror(x) for x in planes(pl.ds(TEAMS * OWN - 8, 8))]
        else:
            after = planes(pl.ds(q * OWN + OWN, 8))
        if q == 0:
            before = [mirror(x) for x in planes(pl.ds(0, 8))]
        else:
            before = planes(pl.ds(q * OWN - 8, 8))
        row = lax.broadcasted_iota(jnp.int32, (8, LANES), 0)
        halo = [jnp.where(row < 4, x, y) for x, y in zip(after, before)]
        put(q, pl.ds(OWN, 8), halo)


def rates(par, t):
    dt_ref, mix_ref, reset_ref = par
    keep = 1.0 - reset_ref[t].astype(jnp.float32)
    return dt_ref[t], keep * (1.0 - mix_ref[t]), keep * mix_ref[t]


def edge_kernel(r1, up_ref, down_ref):
    def tile(s, plane, j):
        return r1[4 * s + j, plane]

    @pl.loop(0, 2)
    def _(comp):
        ua = [tile(0, comp, j) for j in range(BLOCKS)]
        ub = [tile(1, comp, j) for j in range(BLOCKS)]
        for j in range(BLOCKS):
            wa, wb, cb = tile(0, 2 + comp, j), tile(1, 2 + comp, j), tile(1, 4, j)
            down_ref[j, comp] = (laplacian(ua, j) - wa) + (wb - cb * ua[j])
            up_ref[j, comp] = laplacian(ub, j) + (cb * ua[j] - wb)
            up_ref[j, 2 + comp] = ub[j]
            down_ref[j, 2 + comp] = wa

    for j in range(BLOCKS):
        up_ref[j, 4] = tile(1, 4, j)
        down_ref[j, 4] = tile(0, 4, j)
        down_ref[j, 5] = tile(0, 4, j) + tile(1, 4, j)


def product_groups():
    p, f, g, h = [[4 * i + k for k in range(4)] for i in range(4)]
    both = lambda x, y: [(i, k) for i in x for k in y]
    half = lambda x: [(i, k) for i in x for k in x if i <= k]
    return [
        half(p) + both(f, p) + half(f),
        both(g, p) + both(g, f),
        both(h, p) + both(h, f),
        half(g) + both(g, h) + half(h),
    ]


PRODUCTS = [pair for group in product_groups() for pair in group]
SUMS = 256


def force_kernel(
    dt_ref, mix_ref, reset_ref, own_up, own_down, got_up, got_down, v_own, v_up, v_down,
    fgh, sums_ref, x, lv, lf, fs, part,
):
    par = (dt_ref, mix_ref, reset_ref)
    dt0, a0, _ = rates(par, 0)
    dt1, a1, _ = rates(par, 1)
    dt2, a2, _ = rates(par, 2)

    def cross(s, j):
        return (got_up, own_down, own_up, got_down)[s][j, 4]

    def diagonal(s, j):
        if s == 1:
            return own_down[j, 5]
        if s == 3:
            return got_down[j, 5]
        return cross(s, j) + cross(s + 1, j)

    def speed(s, comp, j):
        return (v_up[j, comp], v_own[j, comp], v_own[BLOCKS + j, comp], v_down[j, comp])[s]

    @pl.loop(0, 2)
    def _(comp):
        for j in range(BLOCKS):
            fgh[0, 0, comp, j] = got_up[j, comp] + (own_down[j, 2 + comp] - own_down[j, 4] * got_up[j, 2 + comp])
            fgh[1, 0, comp, j] = own_down[j, comp] + own_down[j, 4] * got_up[j, 2 + comp]
            fgh[2, 0, comp, j] = own_up[j, comp] + (got_down[j, 2 + comp] - got_down[j, 4] * own_up[j, 2 + comp])
            fgh[3, 0, comp, j] = got_down[j, comp] + got_down[j, 4] * own_up[j, 2 + comp]
        for s in range(4):
            v = [speed(s, comp, j) for j in range(BLOCKS)]
            f = [fgh[s, 0, comp, j] for j in range(BLOCKS)]
            for j in range(BLOCKS):
                diag = diagonal(s, j)
                own_v = laplacian(v, j) - diag * v[j]
                own_f = laplacian(f, j) - diag * f[j]
                fgh[s, 1, comp, j] = f[j] + (dt0 * a0) * own_v
                fgh[s, 2, comp, j] = dt0 * own_f
                if s in (1, 2):
                    lv[s - 1, j] = own_v
                    lf[s - 1, j] = own_f
        for s in (1, 2):
            g = [fgh[s, 1, comp, j] for j in range(BLOCKS)]
            h = [fgh[s, 2, comp, j] for j in range(BLOCKS)]
            for j in range(BLOCKS):
                rows = pl.ds(pl.multiple_of(((comp * 2 + (s - 1)) * BLOCKS + j) * OWN, OWN), OWN)
                low, high, diag = cross(s, j), cross(s + 1, j), diagonal(s, j)
                own_v, own_f = lv[s - 1, j], lf[s - 1, j]
                own_g = laplacian(g, j) - diag * g[j]
                own_h = laplacian(h, j) - diag * h[j]

                def put(place, value):
                    x[place, rows] = value[:OWN]

                def other(i):
                    if i < 0:
                        return low * speed(s - 1, comp, j) + high * speed(s + 1, comp, j)
                    return low * fgh[s - 1, i, comp, j] + high * fgh[s + 1, i, comp, j]

                put(0, speed(s, comp, j))
                put(1, fgh[s, 0, comp, j])
                put(2, g[j])
                put(3, h[j])
                out = other(-1)
                f2 = g[j] + (dt1 * a1 * a0) * own_v + (dt0 * a0) * out
                fs[0, j] = f2
                put(4, f2)
                put(8, f2 + (dt2 * a2 * a1 * a0) * own_v + (dt1 * a1 * a0) * out)
                out = other(0)
                f2 = h[j] + (dt1 * a1) * own_f + dt0 * out
                fs[1, j] = f2
                put(5, f2)
                put(9, f2 + (dt2 * a2 * a1) * own_f + (dt1 * a1) * out)
                f2 = dt1 * own_g
                fs[2, j] = f2
                put(6, f2)
                put(10, f2 + (dt2 * a2) * own_g + dt1 * other(1))
                f2 = dt1 * own_h
                fs[3, j] = f2
                put(7, f2)
                put(11, f2 + (dt2 * a2) * own_h + dt1 * other(2))
            for i in range(4):
                f = [fs[i, j] for j in range(BLOCKS)]
                for j in range(BLOCKS):
                    rows = pl.ds(pl.multiple_of(((comp * 2 + (s - 1)) * BLOCKS + j) * OWN, OWN), OWN)
                    x[12 + i, rows] = (dt2 * (laplacian(f, j) - diagonal(s, j) * f[j]))[:OWN]

    part[...] = jnp.zeros_like(part)
    place = 0
    for group in product_groups():
        needed = sorted({i for pair in group for i in pair})

        def body(t, sums):
            rows = pl.ds(pl.multiple_of(t * 8, 8), 8)
            held = {i: x[i, rows] for i in needed}
            return tuple(total + held[i] * held[k] for total, (i, k) in zip(sums, group))

        start = tuple(jnp.zeros((8, LANES), jnp.float32) for _ in group)
        sums = lax.fori_loop(0, x.shape[1] // 8, body, start, unroll=2)
        for total in sums:
            part[pl.ds(place, 1)] = jnp.sum(total, axis=0, keepdims=True)
            place += 1
    row = lax.dot_general(
        jnp.ones((8, LANES), jnp.float32),
        part[...],
        (((1,), (1,)), ((), ())),
        precision=lax.Precision.HIGHEST,
        preferred_element_type=jnp.float32,
    )
    count = min(sums_ref.shape[0], 8)
    for start in range(0, sums_ref.shape[0], count):
        sums_ref[pl.ds(start, count)] = row[:count]


def two_steps(sums, par, t):
    fv, ff, vv, gv, gf, hv, hf, gg, gh, hh = sums
    dt, a, m = rates(par, t)
    b = m * jnp.sqrt(jnp.maximum(vv, 0.0) / (jnp.maximum(ff, 0.0) + EPS)) + dt
    dt_next, a_next, m_next = rates(par, t + 1)
    power_next = a * gv + b * gf + b * (a * hv + b * hf)
    ff_next = jnp.maximum(gg + b * (2.0 * gh + b * hh), 0.0)
    vv_next = jnp.maximum(a * a * vv + b * (2.0 * a * fv + b * ff), 0.0)
    b_next = m_next * jnp.sqrt(vv_next / (ff_next + EPS)) + dt_next
    return (dt, a, b), (dt_next, a_next, b_next), (fv, power_next)


def end_kernel(dt_ref, mix_ref, reset_ref, total_ref, r1, own_up, own_down, got_down, v_own, v_up, v_down, fgh, out_ref, power_ref, v1s, v2s, f2s, v3s):
    par = (dt_ref, mix_ref, reset_ref)
    total = jnp.sum(total_ref[...], axis=0, keepdims=True)
    at = {pair: place for place, pair in enumerate(PRODUCTS)}

    def inner(i, k):
        place = at[(i, k)] if (i, k) in at else at[(k, i)]
        return total[:, place : place + 1]

    v, f, g, h = range(4)
    known = [inner(*pair) for pair in ((f, v), (f, f), (v, v), (g, v), (g, f), (h, v), (h, f), (g, g), (g, h), (h, h))]
    (dt0, a0, b0), (dt1, a1, b1), powers = two_steps(known, par, 0)
    one = jnp.ones_like(b0)
    f_part = [one, b0, b1, b0 * b1]
    v_part = [a1 * a0 * one, a1 * b0, b1, b0 * b1]

    def form(left, i, right, k):
        return sum(
            left[m] * sum(right[n] * inner(4 * i + m, 4 * k + n) for n in range(4)) for m in range(4)
        )

    p, f, g, h = range(4)
    known = [
        form(f_part, f, v_part, p),
        form(f_part, f, f_part, f),
        form(v_part, p, v_part, p),
        form(f_part, g, v_part, p),
        form(f_part, g, f_part, f),
        form(f_part, h, v_part, p),
        form(f_part, h, f_part, f),
        form(f_part, g, f_part, g),
        form(f_part, g, f_part, h),
        form(f_part, h, f_part, h),
    ]
    (dt2, a2, b2), (dt3, a3, b3), later = two_steps(known, par, 2)
    for place, power in enumerate(powers + later):
        power_ref[place] = power[0, 0]

    def cross(s, j):
        return (None, own_down, own_up, got_down)[s][j, 4]

    @pl.loop(0, 2)
    def _(comp):
        for s in range(4):
            for j in range(BLOCKS):
                v0 = (v_up[j, comp], v_own[j, comp], v_own[BLOCKS + j, comp], v_down[j, comp])[s]
                v1 = a0 * v0 + b0 * fgh[s, 0, comp, j]
                f1 = fgh[s, 1, comp, j] + b0 * fgh[s, 2, comp, j]
                v1s[s, j] = v1
                v2s[s, j] = a1 * v1 + b1 * f1
                if s in (1, 2):
                    f2s[s - 1, j] = f1
        for s in (1, 2):
            v2 = [v2s[s, j] for j in range(BLOCKS)]
            for j in range(BLOCKS):
                low, high = cross(s, j), cross(s + 1, j)
                own = laplacian(v2, j) - (low + high) * v2[j]
                f2 = (f2s[s - 1, j] + dt1 * own) + dt0 * (low * v1s[s - 1, j] + high * v1s[s + 1, j])
                f2s[s - 1, j] = f2
                v3s[j] = a2 * v2[j] + b2 * f2
            v3 = [v3s[j] for j in range(BLOCKS)]
            for j in range(BLOCKS):
                low, high = cross(s, j), cross(s + 1, j)
                own = laplacian(v3, j) - (low + high) * v3[j]
                f3 = (f2s[s - 1, j] + dt2 * own) + dt1 * (low * v2s[s - 1, j] + high * v2s[s + 1, j])
                v4 = a3 * v3[j] + b3 * f3
                u = r1[BLOCKS * (s - 1) + j, comp]
                u = ((u + dt0 * v1s[s, j]) + dt1 * v2[j]) + (dt2 * v3[j] + dt3 * v4)
                out_ref[BLOCKS * (s - 1) + j, comp] = u[:OWN]
                out_ref[BLOCKS * (s - 1) + j, 2 + comp] = v4[:OWN]


def unpack_kernel(in_ref, u_ref, v_ref):
    for q in range(TEAMS):
        for comp in range(2):
            u_ref[comp, 0, pl.ds(q * OWN, OWN)] = in_ref[q, comp]
            v_ref[comp, 0, pl.ds(q * OWN, OWN)] = in_ref[q, 2 + comp]


def call(kernel, outs, *args, scalars=0, scratch=(), scalar_outs=()):
    smem = pl.BlockSpec(memory_space=pltpu.SMEM)
    vmem = pl.BlockSpec(memory_space=pltpu.VMEM)
    moved = sum(x.size for x in args) * 4 + sum(functools.reduce(lambda p, n: p * n, o, 1) for o in outs) * 4
    return pl.pallas_call(
        kernel,
        out_shape=[jax.ShapeDtypeStruct(o, jnp.float32) for o in outs],
        in_specs=[smem] * scalars + [vmem] * (len(args) - scalars),
        out_specs=[smem if i in scalar_outs else vmem for i in range(len(outs))],
        scratch_shapes=[pltpu.VMEM(s, jnp.float32) for s in scratch],
        cost_estimate=pl.CostEstimate(flops=moved * 8, bytes_accessed=moved, transcendentals=0),
        compiler_params=pltpu.CompilerParams(vmem_limit_bytes=40 * 1024 * 1024),
    )(*args)


def exchange(x, axes):
    return lax.all_to_all(x, axes, 0, 0, tiled=True)


def upward(x):
    count = lax.axis_size(PAIR)
    return lax.ppermute(x, PAIR, [(i, i + 1) for i in range(count - 1)])


def downward(x):
    count = lax.axis_size(PAIR)
    return lax.ppermute(x, PAIR, [(i + 1, i) for i in range(count - 1)])


def all_sums(rows):
    got = exchange(rows, FIRST)
    count = lax.axis_size(SECOND)
    row = jnp.sum(got, axis=0, keepdims=True)
    return exchange(lax.optimization_barrier(jnp.broadcast_to(row, (count, SUMS))), SECOND)


def per_device(positions, initial_velocity, flow, valid, step_sizes, mixing, resets):
    par = (step_sizes, mixing, resets)
    first, second = call(
        pack_kernel,
        [(TEAMS, 5, ROWS, LANES), (TEAMS, 2, ROWS, LANES)],
        positions,
        initial_velocity,
        flow,
        valid,
    )
    v_own = exchange(second, TEAM)
    v_up = upward(v_own[BLOCKS:])
    v_down = downward(v_own[:BLOCKS])
    r1 = exchange(first, TEAM)
    own_up, own_down = call(edge_kernel, [(BLOCKS, 5, ROWS, LANES), (BLOCKS, 6, ROWS, LANES)], r1)
    got_up = upward(own_up)
    got_down = downward(own_down)
    tile = (BLOCKS, ROWS, LANES)
    fgh, sums = call(
        force_kernel,
        [(4, 3, 2) + tile, (lax.axis_size(FIRST), SUMS)],
        *par,
        own_up,
        own_down,
        got_up,
        got_down,
        v_own,
        v_up,
        v_down,
        scalars=3,
        scratch=[(16, 4 * BLOCKS * OWN, LANES), (2,) + tile, (2,) + tile, (4,) + tile, (SUMS, LANES)],
    )
    total = all_sums(sums)
    packed, power = call(
        end_kernel,
        [(TEAMS, 4, OWN, LANES), (4,)],
        *par,
        total,
        r1,
        own_up,
        own_down,
        got_down,
        v_own,
        v_up,
        v_down,
        fgh,
        scalars=3,
        scalar_outs=(1,),
        scratch=[(4,) + tile, (4,) + tile, (2,) + tile, tile],
    )
    back = exchange(packed, TEAM)
    shape = positions.shape
    final_positions, final_velocity = call(unpack_kernel, [shape, shape], back)
    return final_positions, final_velocity, power


def on_mesh(fine):
    field = P(None, SEC, None, COL)
    return jax.shard_map(
        per_device,
        mesh=fine,
        in_specs=(field, field, field, P(SEC, None, COL), P(), P(), P()),
        out_specs=(field, field, P()),
        check_vma=False,
    )


def solution(mesh):
    return on_mesh(Mesh(mesh.devices.reshape(8, 8, 2, 2, 2), SEC + COL))
```

```python
import functools

import jax
import jax.numpy as jnp
from jax import lax
from jax.experimental import pallas as pl
from jax.experimental.pallas import tpu as pltpu
from jax.sharding import Mesh, PartitionSpec as P


K_INNER = 1.0
K_CROSS = 0.5
EPS = 1e-06

SEC = ("z", "y", "xh")
COL = ("xl", "core")
PAIR = ("z", "y")
TEAM = ("xh", "xl", "core")
FIRST = ("z", "xh", "xl")
SECOND = ("y", "core")

OWN = 64
ROWS = 72
LANES = 128
TEAMS = 8
BLOCKS = 4


def roll(x, shift, axis):
    return pltpu.roll(x, shift % x.shape[axis], axis)


def lane_of(x):
    return lax.broadcasted_iota(jnp.int32, x.shape, len(x.shape) - 1)


def laplacian(tiles, j):
    x = tiles[j]
    lane = lane_of(x)
    before = roll(x, 1, 0)
    after = roll(x, -1, 0)
    if j == 0:
        left = jnp.where(lane == 0, x, roll(x, 1, 1))
    else:
        left = roll(jnp.where(lane == LANES - 1, tiles[j - 1], x), 1, 1)
    if j == BLOCKS - 1:
        right = jnp.where(lane == LANES - 1, x, roll(x, -1, 1))
    else:
        right = roll(jnp.where(lane == 0, tiles[j + 1], x), -1, 1)
    return K_INNER * (((before - x) + (after - x)) + ((left - x) + (right - x)))


def mirror(tile):
    row = lax.broadcasted_iota(jnp.int32, tile.shape, 0)
    tile = roll(tile, 4, 0)
    tile = jnp.where(row % 4 < 2, roll(tile, -2, 0), roll(tile, 2, 0))
    return jnp.where(row % 2 < 1, roll(tile, -1, 0), roll(tile, 1, 0))


def pack_kernel(comp, u_hbm, v_hbm, flow_hbm, valid_hbm, out_ref, u_ref, v_ref, flow_ref, valid_ref, sems):
    lowest = lax.axis_index("z") + lax.axis_index("y") + lax.axis_index("xh") == 0
    strength = jnp.where(lowest, 0.0, K_CROSS).astype(jnp.float32)
    copies = [
        pltpu.make_async_copy(source, target, sems.at[i])
        for i, (source, target) in enumerate(
            (
                (v_hbm.at[comp, 0], v_ref),
                (valid_hbm.at[0], valid_ref),
                (u_hbm.at[comp, 0], u_ref),
                (flow_hbm.at[comp, 0], flow_ref),
            )
        )
    ]
    for copy in copies:
        copy.start()
    for copy in copies:
        copy.wait()

    def planes(rows):
        u = u_ref[rows]
        c = valid_ref[rows].astype(jnp.float32) * strength
        return [u, c * (u - flow_ref[rows]), v_ref[rows], c][: out_ref.shape[1]]

    def put(q, rows, values):
        for place, value in enumerate(values):
            out_ref[q, place, rows] = value

    for q in range(TEAMS):
        put(q, pl.ds(0, OWN), planes(pl.ds(q * OWN, OWN)))
        if q == TEAMS - 1:
            after = [mirror(x) for x in planes(pl.ds(TEAMS * OWN - 8, 8))]
        else:
            after = planes(pl.ds(q * OWN + OWN, 8))
        if q == 0:
            before = [mirror(x) for x in planes(pl.ds(0, 8))]
        else:
            before = planes(pl.ds(q * OWN - 8, 8))
        row = lax.broadcasted_iota(jnp.int32, (8, LANES), 0)
        halo = [jnp.where(row < 4, x, y) for x, y in zip(after, before)]
        put(q, pl.ds(OWN, 8), halo)


def rates(par, t):
    dt_ref, mix_ref, reset_ref = par
    keep = 1.0 - reset_ref[t].astype(jnp.float32)
    return dt_ref[t], keep * (1.0 - mix_ref[t]), keep * mix_ref[t]


def edge_kernel(first, *refs):
    if first:
        mine, up_ref, down_ref = refs
        weights = mine
    else:
        mine, weights, up_ref, down_ref = refs
    ua = [mine[j, 0] for j in range(BLOCKS)]
    ub = [mine[BLOCKS + j, 0] for j in range(BLOCKS)]
    for j in range(BLOCKS):
        wa, wb = mine[j, 1], mine[BLOCKS + j, 1]
        ca, cb = weights[j, 3], weights[BLOCKS + j, 3]
        up_ref[j, 0] = laplacian(ub, j) + (cb * ua[j] - wb)
        up_ref[j, 1] = ub[j]
        up_ref[j, 2] = mine[BLOCKS + j, 2]
        down_ref[j, 0] = (laplacian(ua, j) - wa) + (wb - cb * ua[j])
        down_ref[j, 1] = wa
        down_ref[j, 2] = mine[j, 2]
        if first:
            up_ref[j, 3] = cb
            down_ref[j, 3] = ca
            down_ref[j, 4] = ca + cb


def product_groups():
    p, f, g, h = [[4 * i + k for k in range(4)] for i in range(4)]
    both = lambda x, y: [(i, k) for i in x for k in y]
    half = lambda x: [(i, k) for i in x for k in x if i <= k]
    return [
        half(p) + both(f, p) + half(f),
        both(g, p) + both(g, f),
        both(h, p) + both(h, f),
        half(g) + both(g, h) + half(h),
    ]


PRODUCTS = [pair for group in product_groups() for pair in group]
SUMS = 256


def sections_of(got_up, own_down, own_up, got_down):
    refs = (got_up, own_down, own_up, got_down)

    def cross(s, j):
        return refs[s][j, 3]

    def diagonal(s, j):
        return refs[s][j, 4] if s in (1, 3) else refs[s][j, 3] + refs[s + 1][j, 3]

    return cross, diagonal


def force_kernel(first, dt_ref, mix_ref, reset_ref, *refs):
    got_up, own_down, own_up, got_down = refs[:4]
    if first:
        weights = refs[:4]
        fgh, part, x, lv, lf, fs = refs[4:]
    else:
        weights = refs[4:8]
        given, fgh, sums_ref, x, lv, lf, fs, part = refs[8:]
    par = (dt_ref, mix_ref, reset_ref)
    dt0, a0, _ = rates(par, 0)
    dt1, a1, _ = rates(par, 1)
    dt2, a2, _ = rates(par, 2)
    cross, diagonal = sections_of(*weights)

    def speed(s, j):
        return refs[s][j, 2]

    for j in range(BLOCKS):
        c_low, c_high = cross(1, j), cross(3, j)
        below, above = got_up[j, 1], own_up[j, 1]
        fgh[0, 0, j] = got_up[j, 0] + (own_down[j, 1] - c_low * below)
        fgh[1, 0, j] = own_down[j, 0] + c_low * below
        fgh[2, 0, j] = own_up[j, 0] + (got_down[j, 1] - c_high * above)
        fgh[3, 0, j] = got_down[j, 0] + c_high * above
    for s in range(4):
        v = [speed(s, j) for j in range(BLOCKS)]
        f = [fgh[s, 0, j] for j in range(BLOCKS)]
        for j in range(BLOCKS):
            diag = diagonal(s, j)
            own_v = laplacian(v, j) - diag * v[j]
            own_f = laplacian(f, j) - diag * f[j]
            fgh[s, 1, j] = f[j] + (dt0 * a0) * own_v
            fgh[s, 2, j] = dt0 * own_f
            if s in (1, 2):
                lv[s - 1, j] = own_v
                lf[s - 1, j] = own_f
    for s in (1, 2):
        g = [fgh[s, 1, j] for j in range(BLOCKS)]
        h = [fgh[s, 2, j] for j in range(BLOCKS)]
        for j in range(BLOCKS):
            rows = pl.ds(((s - 1) * BLOCKS + j) * OWN, OWN)
            low, high, diag = cross(s, j), cross(s + 1, j), diagonal(s, j)
            own_v, own_f = lv[s - 1, j], lf[s - 1, j]
            own_g = laplacian(g, j) - diag * g[j]
            own_h = laplacian(h, j) - diag * h[j]

            def put(place, value):
                x[place, rows] = value[:OWN]

            def other(i):
                return low * fgh[s - 1, i, j] + high * fgh[s + 1, i, j]

            put(0, speed(s, j))
            put(1, fgh[s, 0, j])
            put(2, g[j])
            put(3, h[j])
            out = low * speed(s - 1, j) + high * speed(s + 1, j)
            f2 = g[j] + (dt1 * a1 * a0) * own_v + (dt0 * a0) * out
            fs[0, j] = f2
            put(4, f2)
            put(8, f2 + (dt2 * a2 * a1 * a0) * own_v + (dt1 * a1 * a0) * out)
            out = other(0)
            f2 = h[j] + (dt1 * a1) * own_f + dt0 * out
            fs[1, j] = f2
            put(5, f2)
            put(9, f2 + (dt2 * a2 * a1) * own_f + (dt1 * a1) * out)
            f2 = dt1 * own_g
            fs[2, j] = f2
            put(6, f2)
            put(10, f2 + (dt2 * a2) * own_g + dt1 * other(1))
            f2 = dt1 * own_h
            fs[3, j] = f2
            put(7, f2)
            put(11, f2 + (dt2 * a2) * own_h + dt1 * other(2))
        for i in range(4):
            f = [fs[i, j] for j in range(BLOCKS)]
            for j in range(BLOCKS):
                rows = pl.ds(((s - 1) * BLOCKS + j) * OWN, OWN)
                x[12 + i, rows] = (dt2 * (laplacian(f, j) - diagonal(s, j) * f[j]))[:OWN]

    used = len(PRODUCTS)
    part[pl.ds(used, SUMS - used)] = jnp.zeros((SUMS - used, LANES), jnp.float32)
    place = 0
    for group in product_groups():
        needed = sorted({i for pair in group for i in pair})

        def body(t, sums):
            rows = pl.ds(pl.multiple_of(t * 8, 8), 8)
            held = {i: x[i, rows] for i in needed}
            return tuple(total + held[i] * held[k] for total, (i, k) in zip(sums, group))

        start = tuple(jnp.zeros((8, LANES), jnp.float32) for _ in group)
        sums = lax.fori_loop(0, x.shape[1] // 8, body, start, unroll=2)
        for total in sums:
            total = jnp.sum(total, axis=0, keepdims=True)
            part[pl.ds(place, 1)] = total if first else total + given[pl.ds(place, 1)]
            place += 1
    if first:
        return
    row = lax.dot_general(
        jnp.ones((8, LANES), jnp.float32),
        part[...],
        (((1,), (1,)), ((), ())),
        precision=lax.Precision.HIGHEST,
        preferred_element_type=jnp.float32,
    )
    sums_ref[...] = jnp.broadcast_to(row[None, :1], sums_ref.shape)


def add_kernel(in_ref, out_ref):
    out_ref[...] = jnp.broadcast_to(jnp.sum(in_ref[...], axis=0, keepdims=True), out_ref.shape)


def two_steps(sums, par, t):
    fv, ff, vv, gv, gf, hv, hf, gg, gh, hh = sums
    dt, a, m = rates(par, t)
    b = m * jnp.sqrt(jnp.maximum(vv, 0.0) / (jnp.maximum(ff, 0.0) + EPS)) + dt
    dt_next, a_next, m_next = rates(par, t + 1)
    power_next = a * gv + b * gf + b * (a * hv + b * hf)
    ff_next = jnp.maximum(gg + b * (2.0 * gh + b * hh), 0.0)
    vv_next = jnp.maximum(a * a * vv + b * (2.0 * a * fv + b * ff), 0.0)
    b_next = m_next * jnp.sqrt(vv_next / (ff_next + EPS)) + dt_next
    return (dt, a, b), (dt_next, a_next, b_next), (fv, power_next)


def end_kernel(dt_ref, mix_ref, reset_ref, total_ref, *refs):
    u_refs, parts, fghs = refs[:2], (refs[2:6], refs[6:10]), refs[10:12]
    out_ref, power_ref, v1s, v2s, f2s, v3s = refs[12:]
    par = (dt_ref, mix_ref, reset_ref)
    total = jnp.sum(total_ref[...], axis=0)
    at = {pair: place for place, pair in enumerate(PRODUCTS)}

    def inner(i, k):
        place = at[(i, k)] if (i, k) in at else at[(k, i)]
        return total[:, place : place + 1]

    v, f, g, h = range(4)
    known = [inner(*pair) for pair in ((f, v), (f, f), (v, v), (g, v), (g, f), (h, v), (h, f), (g, g), (g, h), (h, h))]
    (dt0, a0, b0), (dt1, a1, b1), powers = two_steps(known, par, 0)
    one = jnp.ones_like(b0)
    f_part = [one, b0, b1, b0 * b1]
    v_part = [a1 * a0 * one, a1 * b0, b1, b0 * b1]

    def form(left, i, right, k):
        return sum(
            left[m] * sum(right[n] * inner(4 * i + m, 4 * k + n) for n in range(4)) for m in range(4)
        )

    p, f, g, h = range(4)
    known = [
        form(f_part, f, v_part, p),
        form(f_part, f, f_part, f),
        form(v_part, p, v_part, p),
        form(f_part, g, v_part, p),
        form(f_part, g, f_part, f),
        form(f_part, h, v_part, p),
        form(f_part, h, f_part, f),
        form(f_part, g, f_part, g),
        form(f_part, g, f_part, h),
        form(f_part, h, f_part, h),
    ]
    (dt2, a2, b2), (dt3, a3, b3), later = two_steps(known, par, 2)
    for place, power in enumerate(powers + later):
        power_ref[place] = power[0, 0]

    cross, diagonal = sections_of(*parts[0])
    for comp in range(2):
        fgh = fghs[comp]
        for s in range(4):
            for j in range(BLOCKS):
                v1 = a0 * parts[comp][s][j, 2] + b0 * fgh[s, 0, j]
                f1 = fgh[s, 1, j] + b0 * fgh[s, 2, j]
                v1s[s, j] = v1
                v2s[s, j] = a1 * v1 + b1 * f1
                if s in (1, 2):
                    f2s[s - 1, j] = f1
        for s in (1, 2):
            v2 = [v2s[s, j] for j in range(BLOCKS)]
            for j in range(BLOCKS):
                low, high, diag = cross(s, j), cross(s + 1, j), diagonal(s, j)
                own = laplacian(v2, j) - diag * v2[j]
                f2 = (f2s[s - 1, j] + dt1 * own) + dt0 * (low * v1s[s - 1, j] + high * v1s[s + 1, j])
                f2s[s - 1, j] = f2
                v3s[j] = a2 * v2[j] + b2 * f2
            v3 = [v3s[j] for j in range(BLOCKS)]
            for j in range(BLOCKS):
                low, high, diag = cross(s, j), cross(s + 1, j), diagonal(s, j)
                own = laplacian(v3, j) - diag * v3[j]
                f3 = (f2s[s - 1, j] + dt2 * own) + dt1 * (low * v2s[s - 1, j] + high * v2s[s + 1, j])
                v4 = a3 * v3[j] + b3 * f3
                u = u_refs[comp][BLOCKS * (s - 1) + j, 0]
                u = ((u + dt0 * v1s[s, j]) + dt1 * v2[j]) + (dt2 * v3[j] + dt3 * v4)
                out_ref[BLOCKS * (s - 1) + j, comp] = u[:OWN]
                out_ref[BLOCKS * (s - 1) + j, 2 + comp] = v4[:OWN]


def unpack_kernel(in_ref, u_ref, v_ref):
    for q in range(TEAMS):
        for comp in range(2):
            u_ref[comp, 0, pl.ds(q * OWN, OWN)] = in_ref[q, comp]
            v_ref[comp, 0, pl.ds(q * OWN, OWN)] = in_ref[q, 2 + comp]


def call(kernel, outs, *args, scalars=0, scratch=(), scalar_outs=(), space=pltpu.VMEM, mib=24):
    smem = pl.BlockSpec(memory_space=pltpu.SMEM)
    vmem = pl.BlockSpec(memory_space=pltpu.VMEM)
    given = pl.BlockSpec(memory_space=space)
    moved = sum(x.size for x in args) * 4 + sum(functools.reduce(lambda p, n: p * n, o, 1) for o in outs) * 4
    return pl.pallas_call(
        kernel,
        out_shape=[jax.ShapeDtypeStruct(o, jnp.float32) for o in outs],
        in_specs=[smem] * scalars + [given] * (len(args) - scalars),
        out_specs=[smem if i in scalar_outs else vmem for i in range(len(outs))],
        scratch_shapes=[pltpu.VMEM(s, jnp.float32) if isinstance(s, tuple) else s for s in scratch],
        cost_estimate=pl.CostEstimate(flops=moved * 8, bytes_accessed=moved, transcendentals=0),
        compiler_params=pltpu.CompilerParams(vmem_limit_bytes=mib * 1024 * 1024),
    )(*args)


def exchange(x, axes):
    return lax.all_to_all(x, axes, 0, 0, tiled=True)


def upward(x):
    count = lax.axis_size(PAIR)
    return lax.ppermute(x, PAIR, [(i, i + 1) for i in range(count - 1)])


def downward(x):
    count = lax.axis_size(PAIR)
    return lax.ppermute(x, PAIR, [(i + 1, i) for i in range(count - 1)])


def all_sums(rows):
    got = exchange(rows, FIRST)
    (row,) = call(add_kernel, [(lax.axis_size(SECOND), 1, SUMS)], got, mib=2)
    return exchange(row, SECOND)


def per_device(positions, initial_velocity, flow, valid, step_sizes, mixing, resets):
    par = (step_sizes, mixing, resets)
    tile = (BLOCKS, ROWS, LANES)
    grid = positions.shape[2:]

    def pack(comp):
        return call(
            functools.partial(pack_kernel, comp),
            [(TEAMS, 4 - comp, ROWS, LANES)],
            positions,
            initial_velocity,
            flow,
            valid,
            scratch=[grid, grid, grid, pltpu.VMEM(grid, jnp.int32), pltpu.SemaphoreType.DMA((4,))],
            space=pl.ANY,
            mib=8,
        )[0]

    def edges(comp, *given):
        return call(
            functools.partial(edge_kernel, comp == 0),
            [(BLOCKS, 4 - comp, ROWS, LANES), (BLOCKS, 5 - 2 * comp, ROWS, LANES)],
            *given,
            mib=8,
        )

    packed = [pack(0), pack(1)]
    mine0 = exchange(packed[0], TEAM)
    up0, down0 = edges(0, mine0)
    packed1, up0, down0 = lax.optimization_barrier((packed[1], up0, down0))
    above0 = downward(down0)
    below0 = upward(up0)
    mine1 = exchange(packed1, TEAM)
    up1, down1 = edges(1, mine1, mine0)
    above1 = downward(down1)
    below1 = upward(up1)

    part0 = (below0, down0, up0, above0)
    part1 = (below1, down1, up1, above1)
    work = [(16, 2 * BLOCKS * OWN, LANES), (2,) + tile, (2,) + tile, (4,) + tile]
    fgh0, sums = call(
        functools.partial(force_kernel, True), [(4, 3) + tile, (SUMS, LANES)], *par, *part0, scalars=3, scratch=work
    )
    fgh1, sums = call(
        functools.partial(force_kernel, False),
        [(4, 3) + tile, (lax.axis_size(FIRST), 1, SUMS)],
        *par,
        *part1,
        *part0,
        sums,
        scalars=3,
        scratch=work + [(SUMS, LANES)],
    )
    total = all_sums(sums)
    packed, power = call(
        end_kernel,
        [(TEAMS, 4, OWN, LANES), (4,)],
        *par,
        total,
        mine0,
        mine1,
        *part0,
        *part1,
        fgh0,
        fgh1,
        scalars=3,
        scalar_outs=(1,),
        scratch=[(4,) + tile, (4,) + tile, (2,) + tile, tile],
    )
    back = exchange(packed, TEAM)
    shape = positions.shape
    final_positions, final_velocity = call(unpack_kernel, [shape, shape], back, mib=8)
    return final_positions, final_velocity, power


def on_mesh(fine):
    field = P(None, SEC, None, COL)
    return jax.shard_map(
        per_device,
        mesh=fine,
        in_specs=(field, field, field, P(SEC, None, COL), P(), P(), P()),
        out_specs=(field, field, P()),
        check_vma=False,
    )


def solution(mesh):
    return on_mesh(Mesh(mesh.devices.reshape(8, 8, 2, 2, 2), SEC + COL))
```

```python
import functools

import jax
import jax.numpy as jnp
from jax import lax
from jax.experimental import pallas as pl
from jax.experimental.pallas import tpu as pltpu
from jax.sharding import Mesh, PartitionSpec as P


K_INNER = 1.0
K_CROSS = 0.5
EPS = 1e-06

SEC = ("z", "y", "xh")
COL = ("xl", "core")
PAIR = ("z", "y")
TEAM = ("xh", "xl", "core")
FIRST = ("z", "xh", "xl")
SECOND = ("y", "core")

OWN = 64
ROWS = 72
LANES = 128
TEAMS = 8
BLOCKS = 4


def roll(x, shift, axis):
    return pltpu.roll(x, shift % x.shape[axis], axis)


def lane_of(x):
    return lax.broadcasted_iota(jnp.int32, x.shape, len(x.shape) - 1)


def laplacian(tiles, j):
    x = tiles[j]
    lane = lane_of(x)
    before = roll(x, 1, 0)
    after = roll(x, -1, 0)
    if j == 0:
        left = jnp.where(lane == 0, x, roll(x, 1, 1))
    else:
        left = roll(jnp.where(lane == LANES - 1, tiles[j - 1], x), 1, 1)
    if j == BLOCKS - 1:
        right = jnp.where(lane == LANES - 1, x, roll(x, -1, 1))
    else:
        right = roll(jnp.where(lane == 0, tiles[j + 1], x), -1, 1)
    return K_INNER * (((before - x) + (after - x)) + ((left - x) + (right - x)))


def mirror(tile):
    row = lax.broadcasted_iota(jnp.int32, tile.shape, 0)
    tile = roll(tile, 4, 0)
    tile = jnp.where(row % 4 < 2, roll(tile, -2, 0), roll(tile, 2, 0))
    return jnp.where(row % 2 < 1, roll(tile, -1, 0), roll(tile, 1, 0))


def pack_kernel(comp, u_hbm, v_hbm, flow_hbm, valid_hbm, out_hbm, out_ref, u_ref, v_ref, flow_ref, valid_ref, sems, out_sems):
    lowest = lax.axis_index("z") + lax.axis_index("y") + lax.axis_index("xh") == 0
    strength = jnp.where(lowest, 0.0, K_CROSS).astype(jnp.float32)
    copies = [
        pltpu.make_async_copy(source, target, sems.at[i])
        for i, (source, target) in enumerate(
            (
                (v_hbm.at[comp, 0], v_ref),
                (valid_hbm.at[0], valid_ref),
                (u_hbm.at[comp, 0], u_ref),
                (flow_hbm.at[comp, 0], flow_ref),
            )
        )
    ]
    for copy in copies:
        copy.start()
    for copy in copies:
        copy.wait()

    def planes(rows):
        u = u_ref[rows]
        c = valid_ref[rows].astype(jnp.float32) * strength
        return [u, c * (u - flow_ref[rows]), v_ref[rows], c][: out_ref.shape[1]]

    def put(q, rows, values):
        for place, value in enumerate(values):
            out_ref[q, place, rows] = value

    for q in range(TEAMS):
        put(q, pl.ds(0, OWN), planes(pl.ds(q * OWN, OWN)))
        if q == TEAMS - 1:
            after = [mirror(x) for x in planes(pl.ds(TEAMS * OWN - 8, 8))]
        else:
            after = planes(pl.ds(q * OWN + OWN, 8))
        if q == 0:
            before = [mirror(x) for x in planes(pl.ds(0, 8))]
        else:
            before = planes(pl.ds(q * OWN - 8, 8))
        row = lax.broadcasted_iota(jnp.int32, (8, LANES), 0)
        halo = [jnp.where(row < 4, x, y) for x, y in zip(after, before)]
        put(q, pl.ds(OWN, 8), halo)
        pltpu.make_async_copy(out_ref.at[q], out_hbm.at[q], out_sems.at[q]).start()
    for q in range(TEAMS):
        pltpu.make_async_copy(out_ref.at[q], out_hbm.at[q], out_sems.at[q]).wait()


def rates(par, t):
    dt_ref, mix_ref, reset_ref = par
    keep = 1.0 - reset_ref[t].astype(jnp.float32)
    return dt_ref[t], keep * (1.0 - mix_ref[t]), keep * mix_ref[t]


def edge_kernel(first, *refs):
    if first:
        mine, up_ref, down_ref = refs
        weights = mine
    else:
        mine, weights, up_ref, down_ref = refs
    ua = [mine[j, 0] for j in range(BLOCKS)]
    ub = [mine[BLOCKS + j, 0] for j in range(BLOCKS)]
    for j in range(BLOCKS):
        wa, wb = mine[j, 1], mine[BLOCKS + j, 1]
        ca, cb = weights[j, 3], weights[BLOCKS + j, 3]
        up_ref[j, 0] = laplacian(ub, j) + (cb * ua[j] - wb)
        up_ref[j, 1] = ub[j]
        up_ref[j, 2] = mine[BLOCKS + j, 2]
        down_ref[j, 0] = (laplacian(ua, j) - wa) + (wb - cb * ua[j])
        down_ref[j, 1] = wa
        down_ref[j, 2] = mine[j, 2]
        if first:
            up_ref[j, 3] = cb
            down_ref[j, 3] = ca
            down_ref[j, 4] = ca + cb


def product_groups():
    p, f, g, h = [[4 * i + k for k in range(4)] for i in range(4)]
    both = lambda x, y: [(i, k) for i in x for k in y]
    half = lambda x: [(i, k) for i in x for k in x if i <= k]
    return [
        half(p) + both(f, p) + half(f),
        both(g, p) + both(g, f),
        both(h, p) + both(h, f),
        half(g) + both(g, h) + half(h),
    ]


PRODUCTS = [pair for group in product_groups() for pair in group]
SUMS = 256


def sections_of(got_up, own_down, own_up, got_down):
    refs = (got_up, own_down, own_up, got_down)

    def cross(s, j):
        return refs[s][j, 3]

    def diagonal(s, j):
        return refs[s][j, 4] if s in (1, 3) else refs[s][j, 3] + refs[s + 1][j, 3]

    return cross, diagonal


def force_kernel(first, dt_ref, mix_ref, reset_ref, *refs):
    got_up, own_down, own_up, got_down = refs[:4]
    if first:
        weights = refs[:4]
        x, part, fgh, lv, lf, fs = refs[4:]
    else:
        weights = refs[4:8]
        given, x, sums_ref, fgh, lv, lf, fs, part = refs[8:]
    par = (dt_ref, mix_ref, reset_ref)
    dt0, a0, _ = rates(par, 0)
    dt1, a1, _ = rates(par, 1)
    dt2, a2, _ = rates(par, 2)
    cross, diagonal = sections_of(*weights)

    def speed(s, j):
        return refs[s][j, 2]

    for j in range(BLOCKS):
        c_low, c_high = cross(1, j), cross(3, j)
        below, above = got_up[j, 1], own_up[j, 1]
        fgh[0, 0, j] = got_up[j, 0] + (own_down[j, 1] - c_low * below)
        fgh[1, 0, j] = own_down[j, 0] + c_low * below
        fgh[2, 0, j] = own_up[j, 0] + (got_down[j, 1] - c_high * above)
        fgh[3, 0, j] = got_down[j, 0] + c_high * above
    for s in range(4):
        v = [speed(s, j) for j in range(BLOCKS)]
        f = [fgh[s, 0, j] for j in range(BLOCKS)]
        for j in range(BLOCKS):
            diag = diagonal(s, j)
            own_v = laplacian(v, j) - diag * v[j]
            own_f = laplacian(f, j) - diag * f[j]
            fgh[s, 1, j] = f[j] + (dt0 * a0) * own_v
            fgh[s, 2, j] = dt0 * own_f
            if s in (1, 2):
                lv[s - 1, j] = own_v
                lf[s - 1, j] = own_f
    for s in (1, 2):
        g = [fgh[s, 1, j] for j in range(BLOCKS)]
        h = [fgh[s, 2, j] for j in range(BLOCKS)]
        for j in range(BLOCKS):
            rows = pl.ds(((s - 1) * BLOCKS + j) * OWN, OWN)
            low, high, diag = cross(s, j), cross(s + 1, j), diagonal(s, j)
            own_v, own_f = lv[s - 1, j], lf[s - 1, j]
            own_g = laplacian(g, j) - diag * g[j]
            own_h = laplacian(h, j) - diag * h[j]

            def put(place, value):
                x[place, rows] = value[:OWN]

            def other(i):
                return low * fgh[s - 1, i, j] + high * fgh[s + 1, i, j]

            put(0, speed(s, j))
            put(1, fgh[s, 0, j])
            put(2, g[j])
            put(3, h[j])
            out = low * speed(s - 1, j) + high * speed(s + 1, j)
            f2 = g[j] + (dt1 * a1 * a0) * own_v + (dt0 * a0) * out
            fs[0, j] = f2
            put(4, f2)
            put(8, f2 + (dt2 * a2 * a1 * a0) * own_v + (dt1 * a1 * a0) * out)
            out = other(0)
            f2 = h[j] + (dt1 * a1) * own_f + dt0 * out
            fs[1, j] = f2
            put(5, f2)
            put(9, f2 + (dt2 * a2 * a1) * own_f + (dt1 * a1) * out)
            f2 = dt1 * own_g
            fs[2, j] = f2
            put(6, f2)
            put(10, f2 + (dt2 * a2) * own_g + dt1 * other(1))
            f2 = dt1 * own_h
            fs[3, j] = f2
            put(7, f2)
            put(11, f2 + (dt2 * a2) * own_h + dt1 * other(2))
        for i in range(4):
            f = [fs[i, j] for j in range(BLOCKS)]
            for j in range(BLOCKS):
                rows = pl.ds(((s - 1) * BLOCKS + j) * OWN, OWN)
                x[12 + i, rows] = (dt2 * (laplacian(f, j) - diagonal(s, j) * f[j]))[:OWN]

    used = len(PRODUCTS)
    part[pl.ds(used, SUMS - used)] = jnp.zeros((SUMS - used, LANES), jnp.float32)
    place = 0
    for group in product_groups():
        needed = sorted({i for pair in group for i in pair})

        def body(t, sums):
            rows = pl.ds(pl.multiple_of(t * 8, 8), 8)
            held = {i: x[i, rows] for i in needed}
            return tuple(total + held[i] * held[k] for total, (i, k) in zip(sums, group))

        start = tuple(jnp.zeros((8, LANES), jnp.float32) for _ in group)
        sums = lax.fori_loop(0, x.shape[1] // 8, body, start, unroll=2)
        for total in sums:
            total = jnp.sum(total, axis=0, keepdims=True)
            part[pl.ds(place, 1)] = total if first else total + given[pl.ds(place, 1)]
            place += 1
    if first:
        return
    row = lax.dot_general(
        jnp.ones((8, LANES), jnp.float32),
        part[...],
        (((1,), (1,)), ((), ())),
        precision=lax.Precision.HIGHEST,
        preferred_element_type=jnp.float32,
    )
    sums_ref[...] = jnp.broadcast_to(row[None, :1], sums_ref.shape)


def add_kernel(in_ref, out_ref):
    out_ref[...] = jnp.broadcast_to(jnp.sum(in_ref[...], axis=0, keepdims=True), out_ref.shape)


def two_steps(sums, par, t):
    fv, ff, vv, gv, gf, hv, hf, gg, gh, hh = sums
    dt, a, m = rates(par, t)
    b = m * jnp.sqrt(jnp.maximum(vv, 0.0) / (jnp.maximum(ff, 0.0) + EPS)) + dt
    dt_next, a_next, m_next = rates(par, t + 1)
    power_next = a * gv + b * gf + b * (a * hv + b * hf)
    ff_next = jnp.maximum(gg + b * (2.0 * gh + b * hh), 0.0)
    vv_next = jnp.maximum(a * a * vv + b * (2.0 * a * fv + b * ff), 0.0)
    b_next = m_next * jnp.sqrt(vv_next / (ff_next + EPS)) + dt_next
    return (dt, a, b), (dt_next, a_next, b_next), (fv, power_next)


def end_kernel(dt_ref, mix_ref, reset_ref, total_ref, *refs):
    u_refs, fields = refs[:2], refs[2:4]
    out_ref, power_ref = refs[4:]
    par = (dt_ref, mix_ref, reset_ref)
    total = jnp.sum(total_ref[...], axis=0)
    at = {pair: place for place, pair in enumerate(PRODUCTS)}

    def inner(i, k):
        place = at[(i, k)] if (i, k) in at else at[(k, i)]
        return total[:, place : place + 1]

    v, f, g, h = range(4)
    known = [inner(*pair) for pair in ((f, v), (f, f), (v, v), (g, v), (g, f), (h, v), (h, f), (g, g), (g, h), (h, h))]
    (dt0, a0, b0), (dt1, a1, b1), powers = two_steps(known, par, 0)
    one = jnp.ones_like(b0)
    f_part = [one, b0, b1, b0 * b1]
    v_part = [a1 * a0 * one, a1 * b0, b1, b0 * b1]

    def form(left, i, right, k):
        return sum(
            left[m] * sum(right[n] * inner(4 * i + m, 4 * k + n) for n in range(4)) for m in range(4)
        )

    p, f, g, h = range(4)
    known = [
        form(f_part, f, v_part, p),
        form(f_part, f, f_part, f),
        form(v_part, p, v_part, p),
        form(f_part, g, v_part, p),
        form(f_part, g, f_part, f),
        form(f_part, h, v_part, p),
        form(f_part, h, f_part, f),
        form(f_part, g, f_part, g),
        form(f_part, g, f_part, h),
        form(f_part, h, f_part, h),
    ]
    (dt2, a2, b2), (dt3, a3, b3), later = two_steps(known, par, 2)
    for place, power in enumerate(powers + later):
        power_ref[place] = power[0, 0]

    v3_part = [a2 * k for k in v_part] + [b2 * k for k in f_part]
    v4_part = [a3 * k for k in v3_part] + [b3 * k for k in f_part] + [b3 * b2 * k for k in f_part]
    u_part = [dt1 * k for k in v_part] + [jnp.zeros_like(one)] * 4
    u_part[0] = u_part[0] + dt0 * a0
    u_part[1] = u_part[1] + dt0 * b0
    u_part = [x + dt2 * y for x, y in zip(u_part, v3_part)]
    shape = (8, LANES)
    v4_part = [jnp.broadcast_to(k, shape) for k in v4_part]
    u_part = [jnp.broadcast_to(k, shape) for k in u_part]

    def combine(coefficients, terms):
        terms = [k * x for k, x in zip(coefficients, terms)]
        while len(terms) > 1:
            terms = [sum(terms[i : i + 2]) for i in range(0, len(terms), 2)]
        return terms[0]

    for comp in range(2):
        for block in range(2 * BLOCKS):

            @pl.loop(0, OWN, step=8, unroll=True)
            def _(row):
                held = [fields[comp][i, pl.ds(block * OWN + row, 8)] for i in range(16)]
                v4 = combine(v4_part, held)
                u3 = u_refs[comp][block, 0, pl.ds(row, 8)] + combine(u_part, held[:8])
                out_ref[block, comp, pl.ds(row, 8)] = u3 + dt3 * v4
                out_ref[block, 2 + comp, pl.ds(row, 8)] = v4


def unpack_kernel(in_ref, u_ref, v_ref):
    for q in range(TEAMS):
        for comp in range(2):
            u_ref[comp, 0, pl.ds(q * OWN, OWN)] = in_ref[q, comp]
            v_ref[comp, 0, pl.ds(q * OWN, OWN)] = in_ref[q, 2 + comp]


def call(kernel, outs, *args, scalars=0, scratch=(), scalar_outs=(), space=pltpu.VMEM, out_space=pltpu.VMEM, mib=16):
    smem = pl.BlockSpec(memory_space=pltpu.SMEM)
    out = pl.BlockSpec(memory_space=out_space)
    given = pl.BlockSpec(memory_space=space)
    moved = sum(x.size for x in args) * 4 + sum(functools.reduce(lambda p, n: p * n, o, 1) for o in outs) * 4
    return pl.pallas_call(
        kernel,
        out_shape=[jax.ShapeDtypeStruct(o, jnp.float32) for o in outs],
        in_specs=[smem] * scalars + [given] * (len(args) - scalars),
        out_specs=[smem if i in scalar_outs else out for i in range(len(outs))],
        scratch_shapes=[pltpu.VMEM(s, jnp.float32) if isinstance(s, tuple) else s for s in scratch],
        cost_estimate=pl.CostEstimate(flops=moved * 8, bytes_accessed=moved, transcendentals=0),
        compiler_params=pltpu.CompilerParams(vmem_limit_bytes=mib * 1024 * 1024),
    )(*args)


def exchange(x, axes):
    return lax.all_to_all(x, axes, 0, 0, tiled=True)


def upward(x):
    count = lax.axis_size(PAIR)
    return lax.ppermute(x, PAIR, [(i, i + 1) for i in range(count - 1)])


def downward(x):
    count = lax.axis_size(PAIR)
    return lax.ppermute(x, PAIR, [(i + 1, i) for i in range(count - 1)])


def all_sums(rows):
    got = exchange(rows, FIRST)
    (row,) = call(add_kernel, [(lax.axis_size(SECOND), 1, SUMS)], got, mib=2)
    return exchange(row, SECOND)


def relax(positions, initial_velocity, flow, valid, step_sizes, mixing, resets):
    par = (step_sizes, mixing, resets)
    tile = (BLOCKS, ROWS, LANES)
    grid = positions.shape[2:]

    def pack(comp):
        return call(
            functools.partial(pack_kernel, comp),
            [(TEAMS, 4 - comp, ROWS, LANES)],
            positions,
            initial_velocity,
            flow,
            valid,
            scratch=[
                (TEAMS, 4 - comp, ROWS, LANES),
                grid,
                grid,
                grid,
                pltpu.VMEM(grid, jnp.int32),
                pltpu.SemaphoreType.DMA((4,)),
                pltpu.SemaphoreType.DMA((TEAMS,)),
            ],
            space=pltpu.HBM,
            out_space=pltpu.HBM,
            mib=61,
        )[0]

    def edges(comp, *given):
        return call(
            functools.partial(edge_kernel, comp == 0),
            [(BLOCKS, 4 - comp, ROWS, LANES), (BLOCKS, 5 - 2 * comp, ROWS, LANES)],
            *given,
            mib=8,
        )

    packed = [pack(0), pack(1)]
    mine0 = exchange(packed[0], TEAM)
    up0, down0 = edges(0, mine0)
    above0 = downward(down0)
    below0 = upward(up0)
    mine1 = exchange(packed[1], TEAM)
    up1, down1 = edges(1, mine1, mine0)
    above1 = downward(down1)
    below1 = upward(up1)

    part0 = (below0, down0, up0, above0)
    part1 = (below1, down1, up1, above1)
    fields = (16, 2 * BLOCKS * OWN, LANES)
    work = [(4, 3) + tile, (2,) + tile, (2,) + tile, (4,) + tile]
    fields0, sums = call(
        functools.partial(force_kernel, True), [fields, (SUMS, LANES)], *par, *part0, scalars=3, scratch=work
    )
    fields1, sums = call(
        functools.partial(force_kernel, False),
        [fields, (lax.axis_size(FIRST), 1, SUMS)],
        *par,
        *part1,
        *part0,
        sums,
        scalars=3,
        scratch=work + [(SUMS, LANES)],
    )
    total = all_sums(sums)
    packed, power = call(
        end_kernel,
        [(TEAMS, 4, OWN, LANES), (4,)],
        *par,
        total,
        mine0,
        mine1,
        fields0,
        fields1,
        scalars=3,
        scalar_outs=(1,),
    )
    back = exchange(packed, TEAM)
    shape = positions.shape
    final_positions, final_velocity = call(unpack_kernel, [shape, shape], back, mib=8)
    return final_positions, final_velocity, power


def on_mesh(fine):
    field = P(None, SEC, None, COL)
    return jax.shard_map(
        relax,
        mesh=fine,
        in_specs=(field, field, field, P(SEC, None, COL), P(), P(), P()),
        out_specs=(field, field, P()),
        check_vma=False,
    )


def solution(mesh):
    step = on_mesh(Mesh(mesh.devices.reshape(8, 8, 2, 2, 2), SEC + COL))
    return step
```

```python
import functools

import jax
import jax.numpy as jnp
from jax import lax
from jax.experimental import pallas as pl
from jax.experimental.pallas import tpu as pltpu
from jax.sharding import Mesh, PartitionSpec as P


K_INNER = 1.0
K_CROSS = 0.5
EPS = 1e-06

SEC = ("z", "y", "xh")
COL = ("xl", "core")
PAIR = ("z", "y")
TEAM = ("xh", "xl", "core")
FIRST = ("z", "xh", "xl")
SECOND = ("y", "core")

OWN = 64
ROWS = 72
LANES = 128
TEAMS = 8
BLOCKS = 4


def roll(x, shift, axis):
    return pltpu.roll(x, shift % x.shape[axis], axis)


def lane_of(x):
    return lax.broadcasted_iota(jnp.int32, x.shape, len(x.shape) - 1)


def laplacian(tiles, j):
    x = tiles[j]
    lane = lane_of(x)
    before = roll(x, 1, 0)
    after = roll(x, -1, 0)
    if j == 0:
        left = jnp.where(lane == 0, x, roll(x, 1, 1))
    else:
        left = roll(jnp.where(lane == LANES - 1, tiles[j - 1], x), 1, 1)
    if j == BLOCKS - 1:
        right = jnp.where(lane == LANES - 1, x, roll(x, -1, 1))
    else:
        right = roll(jnp.where(lane == 0, tiles[j + 1], x), -1, 1)
    return K_INNER * (((before - x) + (after - x)) + ((left - x) + (right - x)))


def mirror(tile):
    row = lax.broadcasted_iota(jnp.int32, tile.shape, 0)
    tile = roll(tile, 4, 0)
    tile = jnp.where(row % 4 < 2, roll(tile, -2, 0), roll(tile, 2, 0))
    return jnp.where(row % 2 < 1, roll(tile, -1, 0), roll(tile, 1, 0))


def pack_kernel(comp, u_hbm, v_hbm, flow_hbm, valid_hbm, out_hbm, out_ref, u_ref, v_ref, flow_ref, valid_ref, sems, out_sems):
    lowest = lax.axis_index("z") + lax.axis_index("y") + lax.axis_index("xh") == 0
    strength = jnp.where(lowest, 0.0, K_CROSS).astype(jnp.float32)
    copies = [
        pltpu.make_async_copy(source, target, sems.at[i])
        for i, (source, target) in enumerate(
            (
                (v_hbm.at[comp, 0], v_ref),
                (valid_hbm.at[0], valid_ref),
                (u_hbm.at[comp, 0], u_ref),
                (flow_hbm.at[comp, 0], flow_ref),
            )
        )
    ]
    for copy in copies:
        copy.start()
    for copy in copies:
        copy.wait()

    def planes(rows):
        u = u_ref[rows]
        c = valid_ref[rows].astype(jnp.float32) * strength
        return [u, c * (u - flow_ref[rows]), v_ref[rows], c][: out_ref.shape[1]]

    def put(q, rows, values):
        for place, value in enumerate(values):
            out_ref[q, place, rows] = value

    for q in range(TEAMS):
        put(q, pl.ds(0, OWN), planes(pl.ds(q * OWN, OWN)))
        if q == TEAMS - 1:
            after = [mirror(x) for x in planes(pl.ds(TEAMS * OWN - 8, 8))]
        else:
            after = planes(pl.ds(q * OWN + OWN, 8))
        if q == 0:
            before = [mirror(x) for x in planes(pl.ds(0, 8))]
        else:
            before = planes(pl.ds(q * OWN - 8, 8))
        row = lax.broadcasted_iota(jnp.int32, (8, LANES), 0)
        halo = [jnp.where(row < 4, x, y) for x, y in zip(after, before)]
        put(q, pl.ds(OWN, 8), halo)
        pltpu.make_async_copy(out_ref.at[q], out_hbm.at[q], out_sems.at[q]).start()
    for q in range(TEAMS):
        pltpu.make_async_copy(out_ref.at[q], out_hbm.at[q], out_sems.at[q]).wait()


def rates(par, t):
    dt_ref, mix_ref, reset_ref = par
    keep = 1.0 - reset_ref[t].astype(jnp.float32)
    return dt_ref[t], keep * (1.0 - mix_ref[t]), keep * mix_ref[t]


def edge_kernel(first, *refs):
    if first:
        mine, up_ref, down_ref = refs
        weights = mine
    else:
        mine, weights, up_ref, down_ref = refs
    ua = [mine[j, 0] for j in range(BLOCKS)]
    ub = [mine[BLOCKS + j, 0] for j in range(BLOCKS)]
    for j in range(BLOCKS):
        wa, wb = mine[j, 1], mine[BLOCKS + j, 1]
        ca, cb = weights[j, 3], weights[BLOCKS + j, 3]
        up_ref[j, 0] = laplacian(ub, j) + (cb * ua[j] - wb)
        up_ref[j, 1] = ub[j]
        up_ref[j, 2] = mine[BLOCKS + j, 2]
        down_ref[j, 0] = (laplacian(ua, j) - wa) + (wb - cb * ua[j])
        down_ref[j, 1] = wa
        down_ref[j, 2] = mine[j, 2]
        if first:
            up_ref[j, 3] = cb
            down_ref[j, 3] = ca
            down_ref[j, 4] = ca + cb


def product_groups():
    p, f, g, h = range(0, 4), range(4, 8), range(8, 10), range(10, 14)
    both = lambda x, y: [(i, k) for i in x for k in y]
    half = lambda x: [(i, k) for i in x for k in x if i <= k]
    return [
        half(p) + both(f, p) + half(f),
        both(g, p) + both(g, f) + both(g, h),
        both(h, p) + both(h, f),
        half(g) + half(h),
    ]


PRODUCTS = [pair for group in product_groups() for pair in group]
SUMS = 128
FIELDS = 14


def sections_of(got_up, own_down, own_up, got_down):
    refs = (got_up, own_down, own_up, got_down)

    def cross(s, j):
        return refs[s][j, 3]

    def diagonal(s, j):
        return refs[s][j, 4] if s in (1, 3) else refs[s][j, 3] + refs[s + 1][j, 3]

    return cross, diagonal


def force_kernel(first, dt_ref, mix_ref, reset_ref, *refs):
    got_up, own_down, own_up, got_down = refs[:4]
    if first:
        weights = refs[:4]
        x, part, fgh, lv, lf, fs = refs[4:]
    else:
        weights = refs[4:8]
        given, x, sums_ref, fgh, lv, lf, fs, part = refs[8:]
    par = (dt_ref, mix_ref, reset_ref)
    dt0, a0, _ = rates(par, 0)
    dt1, a1, _ = rates(par, 1)
    dt2, a2, _ = rates(par, 2)
    cross, diagonal = sections_of(*weights)

    def speed(s, j):
        return refs[s][j, 2]

    for j in range(BLOCKS):
        c_low, c_high = cross(1, j), cross(3, j)
        below, above = got_up[j, 1], own_up[j, 1]
        fgh[0, 0, j] = got_up[j, 0] + (own_down[j, 1] - c_low * below)
        fgh[1, 0, j] = own_down[j, 0] + c_low * below
        fgh[2, 0, j] = own_up[j, 0] + (got_down[j, 1] - c_high * above)
        fgh[3, 0, j] = got_down[j, 0] + c_high * above
    for s in range(4):
        v = [speed(s, j) for j in range(BLOCKS)]
        f = [fgh[s, 0, j] for j in range(BLOCKS)]
        for j in range(BLOCKS):
            diag = diagonal(s, j)
            own_v = laplacian(v, j) - diag * v[j]
            own_f = laplacian(f, j) - diag * f[j]
            fgh[s, 1, j] = f[j] + (dt0 * a0) * own_v
            fgh[s, 2, j] = dt0 * own_f
            if s in (1, 2):
                lv[s - 1, j] = own_v
                lf[s - 1, j] = own_f
    for s in (1, 2):
        g = [fgh[s, 1, j] for j in range(BLOCKS)]
        h = [fgh[s, 2, j] for j in range(BLOCKS)]
        for j in range(BLOCKS):
            rows = pl.ds(((s - 1) * BLOCKS + j) * OWN, OWN)
            low, high, diag = cross(s, j), cross(s + 1, j), diagonal(s, j)
            own_v, own_f = lv[s - 1, j], lf[s - 1, j]
            own_g = laplacian(g, j) - diag * g[j]
            own_h = laplacian(h, j) - diag * h[j]

            def put(place, value):
                x[place, rows] = value[:OWN]

            def other(i):
                return low * fgh[s - 1, i, j] + high * fgh[s + 1, i, j]

            put(0, speed(s, j))
            put(1, fgh[s, 0, j])
            put(2, g[j])
            put(3, h[j])
            out = low * speed(s - 1, j) + high * speed(s + 1, j)
            f2 = g[j] + (dt1 * a1 * a0) * own_v + (dt0 * a0) * out
            fs[0, j] = f2
            put(4, f2)
            out = other(0)
            f2 = h[j] + (dt1 * a1) * own_f + dt0 * out
            fs[1, j] = f2
            put(5, f2)
            f2 = dt1 * own_g
            fs[2, j] = f2
            put(6, f2)
            put(8, f2 + (dt2 * a2) * own_g + dt1 * other(1))
            f2 = dt1 * own_h
            fs[3, j] = f2
            put(7, f2)
            put(9, f2 + (dt2 * a2) * own_h + dt1 * other(2))
        for i in range(4):
            f = [fs[i, j] for j in range(BLOCKS)]
            for j in range(BLOCKS):
                rows = pl.ds(((s - 1) * BLOCKS + j) * OWN, OWN)
                x[10 + i, rows] = (dt2 * (laplacian(f, j) - diagonal(s, j) * f[j]))[:OWN]

    used = len(PRODUCTS)
    part[pl.ds(used, SUMS - used)] = jnp.zeros((SUMS - used, LANES), jnp.float32)
    place = 0
    for group in product_groups():
        needed = sorted({i for pair in group for i in pair})

        def body(t, sums):
            rows = pl.ds(pl.multiple_of(t * 8, 8), 8)
            held = {i: x[i, rows] for i in needed}
            return tuple(total + held[i] * held[k] for total, (i, k) in zip(sums, group))

        start = tuple(jnp.zeros((8, LANES), jnp.float32) for _ in group)
        sums = lax.fori_loop(0, x.shape[1] // 8, body, start, unroll=2)
        for total in sums:
            total = jnp.sum(total, axis=0, keepdims=True)
            part[pl.ds(place, 1)] = total if first else total + given[pl.ds(place, 1)]
            place += 1
    if first:
        return
    row = lax.dot_general(
        jnp.ones((8, LANES), jnp.float32),
        part[...],
        (((1,), (1,)), ((), ())),
        precision=lax.Precision.HIGHEST,
        preferred_element_type=jnp.float32,
    )
    sums_ref[...] = jnp.broadcast_to(row[None, :1], sums_ref.shape)


def add_kernel(in_ref, out_ref):
    out_ref[...] = jnp.broadcast_to(jnp.sum(in_ref[...], axis=0, keepdims=True), out_ref.shape)


def two_steps(sums, par, t):
    fv, ff, vv, gv, gf, hv, hf, gg, gh, hh = sums
    dt, a, m = rates(par, t)
    b = m * jnp.sqrt(jnp.maximum(vv, 0.0) / (jnp.maximum(ff, 0.0) + EPS)) + dt
    dt_next, a_next, m_next = rates(par, t + 1)
    power_next = a * gv + b * gf + b * (a * hv + b * hf)
    ff_next = jnp.maximum(gg + b * (2.0 * gh + b * hh), 0.0)
    vv_next = jnp.maximum(a * a * vv + b * (2.0 * a * fv + b * ff), 0.0)
    b_next = m_next * jnp.sqrt(vv_next / (ff_next + EPS)) + dt_next
    return (dt, a, b), (dt_next, a_next, b_next), (fv, power_next)


def end_kernel(dt_ref, mix_ref, reset_ref, total_ref, *refs):
    u_refs, fields = refs[:2], refs[2:4]
    out_ref, power_ref = refs[4:]
    par = (dt_ref, mix_ref, reset_ref)
    total = jnp.sum(total_ref[...], axis=0)
    at = {pair: place for place, pair in enumerate(PRODUCTS)}

    def inner(i, k):
        place = at[(i, k)] if (i, k) in at else at[(k, i)]
        return total[:, place : place + 1]

    v, f, g, h = range(4)
    known = [inner(*pair) for pair in ((f, v), (f, f), (v, v), (g, v), (g, f), (h, v), (h, f), (g, g), (g, h), (h, h))]
    (dt0, a0, b0), (dt1, a1, b1), powers = two_steps(known, par, 0)
    one = jnp.ones_like(b0)
    dt2, a2, _ = rates(par, 2)
    r = (dt1 * a1) * one / (dt0 * one)
    q = (dt2 * a2 * a1) * one / (dt0 * one)
    common = [one, b0, b1, b0 * b1]
    v_part = dict(enumerate([a1 * a0 * one, a1 * b0, b1, b0 * b1]))
    f_part = {4 + i: k for i, k in enumerate(common)}
    h_part = {10 + i: k for i, k in enumerate(common)}
    g_part = {1: r * r - q, 2: q - r - r * r, 3: b0 * (q - r - r * r), 4: one + r, 5: b0 * (one + r), 8: b1, 9: b0 * b1}

    def form(left, right):
        return sum(k * sum(l * inner(i, n) for n, l in right.items()) for i, k in left.items())

    known = [
        form(*pair)
        for pair in (
            (f_part, v_part),
            (f_part, f_part),
            (v_part, v_part),
            (g_part, v_part),
            (g_part, f_part),
            (h_part, v_part),
            (h_part, f_part),
            (g_part, g_part),
            (g_part, h_part),
            (h_part, h_part),
        )
    ]
    (dt2, a2, b2), (dt3, a3, b3), later = two_steps(known, par, 2)
    for place, power in enumerate(powers + later):
        power_ref[place] = power[0, 0]

    def mix(*terms):
        total = {}
        for scale, part in terms:
            for i, k in part.items():
                total[i] = total[i] + scale * k if i in total else scale * k
        return total

    v3_part = mix((a2, v_part), (b2, f_part))
    v4_part = mix((a3, v3_part), (b3, g_part), (b3 * b2, h_part))
    u_part = mix((dt0, {0: a0 * one, 1: b0}), (dt1, v_part), (dt2, v3_part))
    shape = (8, LANES)
    v4_part = [jnp.broadcast_to(v4_part[i], shape) for i in range(FIELDS)]
    u_part = [jnp.broadcast_to(u_part[i], shape) for i in range(8)]

    def combine(coefficients, terms):
        terms = [k * x for k, x in zip(coefficients, terms)]
        while len(terms) > 1:
            terms = [sum(terms[i : i + 2]) for i in range(0, len(terms), 2)]
        return terms[0]

    for comp in range(2):
        for block in range(2 * BLOCKS):

            @pl.loop(0, OWN, step=8, unroll=True)
            def _(row):
                held = [fields[comp][i, pl.ds(block * OWN + row, 8)] for i in range(FIELDS)]
                v4 = combine(v4_part, held)
                u3 = u_refs[comp][block, 0, pl.ds(row, 8)] + combine(u_part, held[:8])
                out_ref[block, comp, pl.ds(row, 8)] = u3 + dt3 * v4
                out_ref[block, 2 + comp, pl.ds(row, 8)] = v4


def unpack_kernel(in_ref, u_ref, v_ref):
    for q in range(TEAMS):
        for comp in range(2):
            u_ref[comp, 0, pl.ds(q * OWN, OWN)] = in_ref[q, comp]
            v_ref[comp, 0, pl.ds(q * OWN, OWN)] = in_ref[q, 2 + comp]


def call(kernel, outs, *args, scalars=0, scratch=(), scalar_outs=(), space=pltpu.VMEM, out_space=pltpu.VMEM, mib=16):
    smem = pl.BlockSpec(memory_space=pltpu.SMEM)
    out = pl.BlockSpec(memory_space=out_space)
    given = pl.BlockSpec(memory_space=space)
    moved = sum(x.size for x in args) * 4 + sum(functools.reduce(lambda p, n: p * n, o, 1) for o in outs) * 4
    return pl.pallas_call(
        kernel,
        out_shape=[jax.ShapeDtypeStruct(o, jnp.float32) for o in outs],
        in_specs=[smem] * scalars + [given] * (len(args) - scalars),
        out_specs=[smem if i in scalar_outs else out for i in range(len(outs))],
        scratch_shapes=[pltpu.VMEM(s, jnp.float32) if isinstance(s, tuple) else s for s in scratch],
        cost_estimate=pl.CostEstimate(flops=moved * 8, bytes_accessed=moved, transcendentals=0),
        compiler_params=pltpu.CompilerParams(vmem_limit_bytes=mib * 1024 * 1024),
    )(*args)


def exchange(x, axes):
    return lax.all_to_all(x, axes, 0, 0, tiled=True)


def upward(x):
    count = lax.axis_size(PAIR)
    return lax.ppermute(x, PAIR, [(i, i + 1) for i in range(count - 1)])


def downward(x):
    count = lax.axis_size(PAIR)
    return lax.ppermute(x, PAIR, [(i + 1, i) for i in range(count - 1)])


def all_sums(rows):
    got = exchange(rows, FIRST)
    (row,) = call(add_kernel, [(lax.axis_size(SECOND), 1, SUMS)], got, mib=2)
    return exchange(row, SECOND)


def relax(positions, initial_velocity, flow, valid, step_sizes, mixing, resets):
    par = (step_sizes, mixing, resets)
    tile = (BLOCKS, ROWS, LANES)
    grid = positions.shape[2:]

    def pack(comp):
        return call(
            functools.partial(pack_kernel, comp),
            [(TEAMS, 4 - comp, ROWS, LANES)],
            positions,
            initial_velocity,
            flow,
            valid,
            scratch=[
                (TEAMS, 4 - comp, ROWS, LANES),
                grid,
                grid,
                grid,
                pltpu.VMEM(grid, jnp.int32),
                pltpu.SemaphoreType.DMA((4,)),
                pltpu.SemaphoreType.DMA((TEAMS,)),
            ],
            space=pltpu.HBM,
            out_space=pltpu.HBM,
            mib=61,
        )[0]

    def edges(comp, *given):
        return call(
            functools.partial(edge_kernel, comp == 0),
            [(BLOCKS, 4 - comp, ROWS, LANES), (BLOCKS, 5 - 2 * comp, ROWS, LANES)],
            *given,
            mib=8,
        )

    packed = [pack(0), pack(1)]
    mine0 = exchange(packed[0], TEAM)
    up0, down0 = edges(0, mine0)
    above0 = downward(down0)
    below0 = upward(up0)
    mine1 = exchange(packed[1], TEAM)
    up1, down1 = edges(1, mine1, mine0)
    above1 = downward(down1)
    below1 = upward(up1)

    part0 = (below0, down0, up0, above0)
    part1 = (below1, down1, up1, above1)
    fields = (FIELDS, 2 * BLOCKS * OWN, LANES)
    work = [(4, 3) + tile, (2,) + tile, (2,) + tile, (4,) + tile]
    fields0, sums = call(
        functools.partial(force_kernel, True), [fields, (SUMS, LANES)], *par, *part0, scalars=3, scratch=work
    )
    fields1, sums = call(
        functools.partial(force_kernel, False),
        [fields, (lax.axis_size(FIRST), 1, SUMS)],
        *par,
        *part1,
        *part0,
        sums,
        scalars=3,
        scratch=work + [(SUMS, LANES)],
    )
    total = all_sums(sums)
    packed, power = call(
        end_kernel,
        [(TEAMS, 4, OWN, LANES), (4,)],
        *par,
        total,
        mine0,
        mine1,
        fields0,
        fields1,
        scalars=3,
        scalar_outs=(1,),
    )
    back = exchange(packed, TEAM)
    shape = positions.shape
    final_positions, final_velocity = call(unpack_kernel, [shape, shape], back, mib=8)
    return final_positions, final_velocity, power


def on_mesh(fine):
    field = P(None, SEC, None, COL)
    return jax.shard_map(
        relax,
        mesh=fine,
        in_specs=(field, field, field, P(SEC, None, COL), P(), P(), P()),
        out_specs=(field, field, P()),
        check_vma=False,
    )


def solution(mesh):
    step = on_mesh(Mesh(mesh.devices.reshape(8, 8, 2, 2, 2), SEC + COL))
    return step
```

```python
import functools

import jax
import jax.numpy as jnp
from jax import lax
from jax.experimental import pallas as pl
from jax.experimental.pallas import tpu as pltpu
from jax.sharding import Mesh, PartitionSpec as P


K_INNER = 1.0
K_CROSS = 0.5
EPS = 1e-06

SEC = ("z", "y", "xh")
COL = ("xl", "core")
PAIR = ("z", "y")
TEAM = ("xh", "xl", "core")
FIRST = ("z", "xh", "xl")
SECOND = ("y", "core")

OWN = 64
ROWS = 72
LANES = 128
TEAMS = 8
BLOCKS = 4


def roll(x, shift, axis):
    return pltpu.roll(x, shift % x.shape[axis], axis)


def lane_of(x):
    return lax.broadcasted_iota(jnp.int32, x.shape, len(x.shape) - 1)


def laplacian(tiles, j):
    x = tiles[j]
    lane = lane_of(x)
    before = roll(x, 1, 0)
    after = roll(x, -1, 0)
    if j == 0:
        left = jnp.where(lane == 0, x, roll(x, 1, 1))
    else:
        left = roll(jnp.where(lane == LANES - 1, tiles[j - 1], x), 1, 1)
    if j == BLOCKS - 1:
        right = jnp.where(lane == LANES - 1, x, roll(x, -1, 1))
    else:
        right = roll(jnp.where(lane == 0, tiles[j + 1], x), -1, 1)
    return K_INNER * (((before - x) + (after - x)) + ((left - x) + (right - x)))


def mirror(tile):
    row = lax.broadcasted_iota(jnp.int32, tile.shape, 0)
    tile = roll(tile, 4, 0)
    tile = jnp.where(row % 4 < 2, roll(tile, -2, 0), roll(tile, 2, 0))
    return jnp.where(row % 2 < 1, roll(tile, -1, 0), roll(tile, 1, 0))


def pack_kernel(comp, u_hbm, v_hbm, flow_hbm, valid_hbm, out_hbm, out_ref, u_ref, v_ref, flow_ref, valid_ref, sems, out_sems):
    lowest = lax.axis_index("z") + lax.axis_index("y") + lax.axis_index("xh") == 0
    strength = jnp.where(lowest, 0.0, K_CROSS).astype(jnp.float32)
    copies = [
        pltpu.make_async_copy(source, target, sems.at[i])
        for i, (source, target) in enumerate(
            (
                (v_hbm.at[comp, 0], v_ref),
                (valid_hbm.at[0], valid_ref),
                (u_hbm.at[comp, 0], u_ref),
                (flow_hbm.at[comp, 0], flow_ref),
            )
        )
    ]
    for copy in copies:
        copy.start()
    for copy in copies:
        copy.wait()

    def planes(rows):
        u = u_ref[rows]
        c = valid_ref[rows].astype(jnp.float32) * strength
        return [u, c * (u - flow_ref[rows]), v_ref[rows], c][: out_ref.shape[1]]

    def put(q, rows, values):
        for place, value in enumerate(values):
            out_ref[q, place, rows] = value

    for q in range(TEAMS):
        put(q, pl.ds(0, OWN), planes(pl.ds(q * OWN, OWN)))
        if q == TEAMS - 1:
            after = [mirror(x) for x in planes(pl.ds(TEAMS * OWN - 8, 8))]
        else:
            after = planes(pl.ds(q * OWN + OWN, 8))
        if q == 0:
            before = [mirror(x) for x in planes(pl.ds(0, 8))]
        else:
            before = planes(pl.ds(q * OWN - 8, 8))
        row = lax.broadcasted_iota(jnp.int32, (8, LANES), 0)
        halo = [jnp.where(row < 4, x, y) for x, y in zip(after, before)]
        put(q, pl.ds(OWN, 8), halo)
        pltpu.make_async_copy(out_ref.at[q], out_hbm.at[q], out_sems.at[q]).start()
    for q in range(TEAMS):
        pltpu.make_async_copy(out_ref.at[q], out_hbm.at[q], out_sems.at[q]).wait()


def rates(par, t):
    dt_ref, mix_ref, reset_ref = par
    keep = 1.0 - reset_ref[t].astype(jnp.float32)
    return dt_ref[t], keep * (1.0 - mix_ref[t]), keep * mix_ref[t]


def edge_kernel(first, *refs):
    if first:
        mine, up_ref, down_ref = refs
        weights = mine
    else:
        mine, weights, up_ref, down_ref = refs
    ua = [mine[j, 0] for j in range(BLOCKS)]
    ub = [mine[BLOCKS + j, 0] for j in range(BLOCKS)]
    for j in range(BLOCKS):
        wa, wb = mine[j, 1], mine[BLOCKS + j, 1]
        ca, cb = weights[j, 3], weights[BLOCKS + j, 3]
        up_ref[j, 0] = laplacian(ub, j) + (cb * ua[j] - wb)
        up_ref[j, 1] = ub[j]
        up_ref[j, 2] = mine[BLOCKS + j, 2]
        down_ref[j, 0] = (laplacian(ua, j) - wa) + (wb - cb * ua[j])
        down_ref[j, 1] = wa
        down_ref[j, 2] = mine[j, 2]
        if first:
            up_ref[j, 3] = cb
            down_ref[j, 3] = ca
            down_ref[j, 4] = ca + cb


def product_groups():
    p, f, g, h = range(0, 4), range(4, 8), range(8, 10), range(10, 14)
    both = lambda x, y: [(i, k) for i in x for k in y]
    half = lambda x: [(i, k) for i in x for k in x if i <= k]
    return [
        half(p) + both(f, p) + half(f),
        both(g, p) + both(g, f) + both(g, h),
        [(i, k) for i in h for k in f if i - 10 <= k - 4] + half(g) + half(h),
    ]


PRODUCTS = [pair for group in product_groups() for pair in group]
SUMS = 128
FIELDS = 14


def sections_of(got_up, own_down, own_up, got_down):
    refs = (got_up, own_down, own_up, got_down)

    def cross(s, j):
        return refs[s][j, 3]

    def diagonal(s, j):
        return refs[s][j, 4] if s in (1, 3) else refs[s][j, 3] + refs[s + 1][j, 3]

    return cross, diagonal


def force_kernel(first, dt_ref, mix_ref, reset_ref, *refs):
    got_up, own_down, own_up, got_down = refs[:4]
    if first:
        weights = refs[:4]
        x, part, fgh, lv, lf, fs = refs[4:]
    else:
        weights = refs[4:8]
        given, x, sums_ref, fgh, lv, lf, fs, part = refs[8:]
    par = (dt_ref, mix_ref, reset_ref)
    dt0, a0, _ = rates(par, 0)
    dt1, a1, _ = rates(par, 1)
    dt2, a2, _ = rates(par, 2)
    cross, diagonal = sections_of(*weights)

    def speed(s, j):
        return refs[s][j, 2]

    for j in range(BLOCKS):
        c_low, c_high = cross(1, j), cross(3, j)
        below, above = got_up[j, 1], own_up[j, 1]
        fgh[0, 0, j] = got_up[j, 0] + (own_down[j, 1] - c_low * below)
        fgh[1, 0, j] = own_down[j, 0] + c_low * below
        fgh[2, 0, j] = own_up[j, 0] + (got_down[j, 1] - c_high * above)
        fgh[3, 0, j] = got_down[j, 0] + c_high * above
    for s in range(4):
        v = [speed(s, j) for j in range(BLOCKS)]
        f = [fgh[s, 0, j] for j in range(BLOCKS)]
        for j in range(BLOCKS):
            diag = diagonal(s, j)
            own_v = laplacian(v, j) - diag * v[j]
            own_f = laplacian(f, j) - diag * f[j]
            fgh[s, 1, j] = f[j] + (dt0 * a0) * own_v
            fgh[s, 2, j] = dt0 * own_f
            if s in (1, 2):
                lv[s - 1, j] = own_v
                lf[s - 1, j] = own_f
    for s in (1, 2):
        g = [fgh[s, 1, j] for j in range(BLOCKS)]
        h = [fgh[s, 2, j] for j in range(BLOCKS)]
        for j in range(BLOCKS):
            rows = pl.ds(((s - 1) * BLOCKS + j) * OWN, OWN)
            low, high, diag = cross(s, j), cross(s + 1, j), diagonal(s, j)
            own_v, own_f = lv[s - 1, j], lf[s - 1, j]
            own_g = laplacian(g, j) - diag * g[j]
            own_h = laplacian(h, j) - diag * h[j]

            def put(place, value):
                x[place, rows] = value[:OWN]

            def other(i):
                return low * fgh[s - 1, i, j] + high * fgh[s + 1, i, j]

            put(0, speed(s, j))
            put(1, fgh[s, 0, j])
            put(2, g[j])
            put(3, h[j])
            out = low * speed(s - 1, j) + high * speed(s + 1, j)
            f2 = g[j] + (dt1 * a1 * a0) * own_v + (dt0 * a0) * out
            fs[0, j] = f2
            put(4, f2)
            out = other(0)
            f2 = h[j] + (dt1 * a1) * own_f + dt0 * out
            fs[1, j] = f2
            put(5, f2)
            f2 = dt1 * own_g
            fs[2, j] = f2
            put(6, f2)
            put(8, f2 + (dt2 * a2) * own_g + dt1 * other(1))
            f2 = dt1 * own_h
            fs[3, j] = f2
            put(7, f2)
            put(9, f2 + (dt2 * a2) * own_h + dt1 * other(2))
        for i in range(4):
            f = [fs[i, j] for j in range(BLOCKS)]
            for j in range(BLOCKS):
                rows = pl.ds(((s - 1) * BLOCKS + j) * OWN, OWN)
                x[10 + i, rows] = (dt2 * (laplacian(f, j) - diagonal(s, j) * f[j]))[:OWN]

    used = len(PRODUCTS)
    part[pl.ds(used, SUMS - used)] = jnp.zeros((SUMS - used, LANES), jnp.float32)
    place = 0
    for group in product_groups():
        needed = sorted({i for pair in group for i in pair})

        def body(t, sums):
            rows = pl.ds(pl.multiple_of(t * 8, 8), 8)
            held = {i: x[i, rows] for i in needed}
            return tuple(total + held[i] * held[k] for total, (i, k) in zip(sums, group))

        start = tuple(jnp.zeros((8, LANES), jnp.float32) for _ in group)
        sums = lax.fori_loop(0, x.shape[1] // 8, body, start, unroll=2)
        for total in sums:
            total = jnp.sum(total, axis=0, keepdims=True)
            part[pl.ds(place, 1)] = total if first else total + given[pl.ds(place, 1)]
            place += 1
    if first:
        return
    row = lax.dot_general(
        jnp.ones((8, LANES), jnp.float32),
        part[...],
        (((1,), (1,)), ((), ())),
        precision=lax.Precision.HIGHEST,
        preferred_element_type=jnp.float32,
    )
    sums_ref[...] = jnp.broadcast_to(row[None, :1], sums_ref.shape)


def add_kernel(in_ref, out_ref):
    out_ref[...] = jnp.broadcast_to(jnp.sum(in_ref[...], axis=0, keepdims=True), out_ref.shape)


def two_steps(sums, par, t):
    fv, ff, vv, gv, gf, hv, hf, gg, gh, hh = sums
    dt, a, m = rates(par, t)
    b = m * jnp.sqrt(jnp.maximum(vv, 0.0) / (jnp.maximum(ff, 0.0) + EPS)) + dt
    dt_next, a_next, m_next = rates(par, t + 1)
    power_next = a * gv + b * gf + b * (a * hv + b * hf)
    ff_next = jnp.maximum(gg + b * (2.0 * gh + b * hh), 0.0)
    vv_next = jnp.maximum(a * a * vv + b * (2.0 * a * fv + b * ff), 0.0)
    b_next = m_next * jnp.sqrt(vv_next / (ff_next + EPS)) + dt_next
    return (dt, a, b), (dt_next, a_next, b_next), (fv, power_next)


def end_kernel(dt_ref, mix_ref, reset_ref, total_ref, *refs):
    u_refs, fields = refs[:2], refs[2:4]
    out_ref, power_ref = refs[4:]
    par = (dt_ref, mix_ref, reset_ref)
    total = jnp.sum(total_ref[...], axis=0)
    at = {pair: place for place, pair in enumerate(PRODUCTS)}

    (near, a, _), (mid, _, _), (far, _, _) = [rates(par, t) for t in range(3)]
    unit = jnp.ones((1, 1), jnp.float32)

    def inner(i, k):
        i, k = max(i, k), min(i, k)
        if i >= 10 and k == 0:
            return (far * unit / (near * a * unit)) * (inner(i - 6, 2) - inner(i - 6, 1))
        if i >= 10 and k < 4:
            return (far * unit / ((near if k == 1 else mid) * unit)) * inner(i - 6, (0, 3, 6, 7)[k])
        if i >= 10 and 4 <= k < 8:
            i, k = 10 + min(i - 10, k - 4), 4 + max(i - 10, k - 4)
        place = at[(i, k)] if (i, k) in at else at[(k, i)]
        return total[:, place : place + 1]

    v, f, g, h = range(4)
    known = [inner(*pair) for pair in ((f, v), (f, f), (v, v), (g, v), (g, f), (h, v), (h, f), (g, g), (g, h), (h, h))]
    (dt0, a0, b0), (dt1, a1, b1), powers = two_steps(known, par, 0)
    one = jnp.ones_like(b0)
    dt2, a2, _ = rates(par, 2)
    r = (dt1 * a1) * one / (dt0 * one)
    q = (dt2 * a2 * a1) * one / (dt0 * one)
    common = [one, b0, b1, b0 * b1]
    v_part = dict(enumerate([a1 * a0 * one, a1 * b0, b1, b0 * b1]))
    f_part = {4 + i: k for i, k in enumerate(common)}
    h_part = {10 + i: k for i, k in enumerate(common)}
    g_part = {1: r * r - q, 2: q - r - r * r, 3: b0 * (q - r - r * r), 4: one + r, 5: b0 * (one + r), 8: b1, 9: b0 * b1}

    def form(left, right):
        return sum(k * sum(l * inner(i, n) for n, l in right.items()) for i, k in left.items())

    known = [
        form(*pair)
        for pair in (
            (f_part, v_part),
            (f_part, f_part),
            (v_part, v_part),
            (g_part, v_part),
            (g_part, f_part),
            (h_part, v_part),
            (h_part, f_part),
            (g_part, g_part),
            (g_part, h_part),
            (h_part, h_part),
        )
    ]
    (dt2, a2, b2), (dt3, a3, b3), later = two_steps(known, par, 2)
    for place, power in enumerate(powers + later):
        power_ref[place] = power[0, 0]

    def mix(*terms):
        total = {}
        for scale, part in terms:
            for i, k in part.items():
                total[i] = total[i] + scale * k if i in total else scale * k
        return total

    v3_part = mix((a2, v_part), (b2, f_part))
    v4_part = mix((a3, v3_part), (b3, g_part), (b3 * b2, h_part))
    u_part = mix((dt0, {0: a0 * one, 1: b0}), (dt1, v_part), (dt2, v3_part))
    shape = (8, LANES)
    v4_part = [jnp.broadcast_to(v4_part[i], shape) for i in range(FIELDS)]
    u_part = [jnp.broadcast_to(u_part[i], shape) for i in range(8)]

    def combine(coefficients, terms):
        terms = [k * x for k, x in zip(coefficients, terms)]
        while len(terms) > 1:
            terms = [sum(terms[i : i + 2]) for i in range(0, len(terms), 2)]
        return terms[0]

    for comp in range(2):
        for block in range(2 * BLOCKS):

            @pl.loop(0, OWN, step=8, unroll=True)
            def _(row):
                held = [fields[comp][i, pl.ds(block * OWN + row, 8)] for i in range(FIELDS)]
                v4 = combine(v4_part, held)
                u3 = u_refs[comp][block, 0, pl.ds(row, 8)] + combine(u_part, held[:8])
                out_ref[block, comp, pl.ds(row, 8)] = u3 + dt3 * v4
                out_ref[block, 2 + comp, pl.ds(row, 8)] = v4


def unpack_kernel(in_ref, u_ref, v_ref):
    for q in range(TEAMS):
        for comp in range(2):
            u_ref[comp, 0, pl.ds(q * OWN, OWN)] = in_ref[q, comp]
            v_ref[comp, 0, pl.ds(q * OWN, OWN)] = in_ref[q, 2 + comp]


def call(kernel, outs, *args, scalars=0, scratch=(), scalar_outs=(), space=pltpu.VMEM, out_space=pltpu.VMEM, mib=16):
    smem = pl.BlockSpec(memory_space=pltpu.SMEM)
    out = pl.BlockSpec(memory_space=out_space)
    given = pl.BlockSpec(memory_space=space)
    moved = sum(x.size for x in args) * 4 + sum(functools.reduce(lambda p, n: p * n, o, 1) for o in outs) * 4
    return pl.pallas_call(
        kernel,
        out_shape=[jax.ShapeDtypeStruct(o, jnp.float32) for o in outs],
        in_specs=[smem] * scalars + [given] * (len(args) - scalars),
        out_specs=[smem if i in scalar_outs else out for i in range(len(outs))],
        scratch_shapes=[pltpu.VMEM(s, jnp.float32) if isinstance(s, tuple) else s for s in scratch],
        cost_estimate=pl.CostEstimate(flops=moved * 8, bytes_accessed=moved, transcendentals=0),
        compiler_params=pltpu.CompilerParams(vmem_limit_bytes=mib * 1024 * 1024),
    )(*args)


def exchange(x, axes):
    return lax.all_to_all(x, axes, 0, 0, tiled=True)


def upward(x):
    count = lax.axis_size(PAIR)
    return lax.ppermute(x, PAIR, [(i, i + 1) for i in range(count - 1)])


def downward(x):
    count = lax.axis_size(PAIR)
    return lax.ppermute(x, PAIR, [(i + 1, i) for i in range(count - 1)])


def all_sums(rows):
    got = exchange(rows, FIRST)
    (row,) = call(add_kernel, [(lax.axis_size(SECOND), 1, SUMS)], got, mib=2)
    return exchange(row, SECOND)


def relax(positions, initial_velocity, flow, valid, step_sizes, mixing, resets):
    par = (step_sizes, mixing, resets)
    tile = (BLOCKS, ROWS, LANES)
    grid = positions.shape[2:]

    def pack(comp):
        return call(
            functools.partial(pack_kernel, comp),
            [(TEAMS, 4 - comp, ROWS, LANES)],
            positions,
            initial_velocity,
            flow,
            valid,
            scratch=[
                (TEAMS, 4 - comp, ROWS, LANES),
                grid,
                grid,
                grid,
                pltpu.VMEM(grid, jnp.int32),
                pltpu.SemaphoreType.DMA((4,)),
                pltpu.SemaphoreType.DMA((TEAMS,)),
            ],
            space=pltpu.HBM,
            out_space=pltpu.HBM,
            mib=61,
        )[0]

    def edges(comp, *given):
        return call(
            functools.partial(edge_kernel, comp == 0),
            [(BLOCKS, 4 - comp, ROWS, LANES), (BLOCKS, 5 - 2 * comp, ROWS, LANES)],
            *given,
            mib=8,
        )

    packed = [pack(0), pack(1)]
    mine0 = exchange(packed[0], TEAM)
    up0, down0 = edges(0, mine0)
    above0 = downward(down0)
    below0 = upward(up0)
    mine1 = exchange(packed[1], TEAM)
    up1, down1 = edges(1, mine1, mine0)
    above1 = downward(down1)
    below1 = upward(up1)

    part0 = (below0, down0, up0, above0)
    part1 = (below1, down1, up1, above1)
    fields = (FIELDS, 2 * BLOCKS * OWN, LANES)
    work = [(4, 3) + tile, (2,) + tile, (2,) + tile, (4,) + tile]
    fields0, sums = call(
        functools.partial(force_kernel, True), [fields, (SUMS, LANES)], *par, *part0, scalars=3, scratch=work
    )
    fields1, sums = call(
        functools.partial(force_kernel, False),
        [fields, (lax.axis_size(FIRST), 1, SUMS)],
        *par,
        *part1,
        *part0,
        sums,
        scalars=3,
        scratch=work + [(SUMS, LANES)],
    )
    total = all_sums(sums)
    packed, power = call(
        end_kernel,
        [(TEAMS, 4, OWN, LANES), (4,)],
        *par,
        total,
        mine0,
        mine1,
        fields0,
        fields1,
        scalars=3,
        scalar_outs=(1,),
    )
    back = exchange(packed, TEAM)
    shape = positions.shape
    final_positions, final_velocity = call(unpack_kernel, [shape, shape], back, mib=8)
    return final_positions, final_velocity, power


def on_mesh(fine):
    field = P(None, SEC, None, COL)
    return jax.shard_map(
        relax,
        mesh=fine,
        in_specs=(field, field, field, P(SEC, None, COL), P(), P(), P()),
        out_specs=(field, field, P()),
        check_vma=False,
    )


def solution(mesh):
    step = on_mesh(Mesh(mesh.devices.reshape(8, 8, 2, 2, 2), SEC + COL))
    return step
```
